32 devices in a mesh: gen: 4 (over x, core), join: 8 (over z, y).
Axes of the slice: x: 2, y: 2, z: 4, core: 2. Of those that a mesh axis runs over, the one named last changes fastest.
Arguments:
- src_emb: bfloat16 [65536, 512], P(('gen', 'join')), may hold values from -64 to 64
- counts: int32 [32, 32], P(('gen', 'join')), may hold values from 0 to 64, as said below
Outputs:
- dup_weight: float32 [65536], P(('gen', 'join'))
The draws below stay inside these ranges and needn't reach their ends.
Inputs may be any that keep to these rules, and one draw needn't show every extreme that they name: Slot c of source s for owner o is live when c < counts[s, o]; in every draw some owner receives 64 live slots from every source.
All inputs are finite; a program needn't handle non-finite values.
Results may differ from the reference program's by a relative error of at most 0.0016.
Values may be sent and summed in bfloat16 or wider, within the bound.
A program may use at most 64 MiB of HBM per device.

```python
import math
import jax
import jax.numpy as jnp
from jax import lax

D = 512
BLOCK = 2048
ROUNDS = 3
NODES = 32
CAP = 64
ROWS = 65536
N_GEN = 4
N_JOIN = 8


def draw_src_emb(key, part):
    keys = jax.random.split(key, 4)
    clusters = max(ROWS // 16, 1)
    centers = jnp.clip(jax.random.normal(keys[0], (clusters, D), jnp.float32), -4.0, 4.0)
    members = jax.random.randint(keys[1], (ROWS,), 0, clusters)
    noise = 0.4 * jnp.clip(jax.random.normal(keys[2], (ROWS, D), jnp.float32), -6.0, 6.0)
    scale = jnp.exp(jax.random.uniform(keys[3], (ROWS, 1), jnp.float32, math.log(0.5), math.log(5.0)))
    values = (centers[members] + noise) * scale
    return values.astype(jnp.bfloat16)


def draw_counts(key, part):
    keys = jax.random.split(key, 5)
    lowest = max(1, CAP * 5 // 8)
    limits = jax.random.randint(keys[0], (NODES,), lowest, CAP + 1)
    raw = jax.random.randint(keys[1], (NODES, NODES), 0, 1048576)
    drawn = limits[None, :] - raw % (limits[None, :] // 2 + 1)
    full_owner = jax.random.randint(keys[2], (), 0, NODES)
    empty_source = jax.random.randint(keys[3], (), 0, NODES)
    empty_owner = (full_owner + 1 + jax.random.randint(keys[4], (), 0, NODES - 1)) % NODES
    column = lax.broadcasted_iota(jnp.int32, (NODES, NODES), 1)
    row = lax.broadcasted_iota(jnp.int32, (NODES, NODES), 0)
    result = jnp.where(column == full_owner, CAP, drawn)
    result = jnp.where((row == empty_source) & (column == empty_owner), 0, result)
    return result.astype(jnp.int32)


def setup_inputs(seed: int = 0) -> dict:
    key_of = jax.random.split(jax.random.key(seed), 3)
    return {
        "src_emb": draw_src_emb(jax.random.fold_in(key_of[2], 71), 0),
        "counts": draw_counts(jax.random.fold_in(key_of[2], 71), 0),
    }


def normalize(src_emb):
    values = src_emb.astype(jnp.float32)
    scaled = values * lax.rsqrt(lax.optimization_barrier(jnp.mean(values * values, axis=1, keepdims=True)) + 1e-06) / math.sqrt(D)
    return scaled.astype(jnp.bfloat16)

def tile_sums(left_rows, left_live, right_rows, right_live):
    scores = jnp.dot(left_rows, right_rows.T, preferred_element_type=jnp.float32)
    kernel = jnp.exp(8.0 * (scores - 1.0))
    return (lax.optimization_barrier(jnp.sum(kernel * right_live[None, :], axis=1)), lax.optimization_barrier(jnp.sum(kernel * left_live[:, None], axis=0)))

def own_tile(operands):
    return tile_sums(operands[0], operands[1], operands[0], operands[1])[0]

def cross_tile(operands):
    return tile_sums(operands[0], operands[1], operands[2], operands[3])

def flatten(array):
    return array.reshape((NODES,) + array.shape[2:])

def reference(src_emb, counts):
    unit = normalize(src_emb)
    blocks = unit.reshape(NODES, NODES, CAP, D).transpose(1, 0, 2, 3).reshape(N_GEN, N_JOIN, BLOCK, D)
    slot_index = jnp.arange(CAP).astype(jnp.int32)
    live = (slot_index[None, None, :] < counts[:, :, None]).astype(jnp.float32)
    live = live.transpose(1, 0, 2).reshape(N_GEN, N_JOIN, BLOCK)
    density = lax.map(own_tile, (flatten(blocks), flatten(live))).reshape(N_GEN, N_JOIN, BLOCK)
    for offset in range(1, ROUNDS + 1):
        moved_blocks = jnp.roll(blocks, offset, axis=1)
        moved_live = jnp.roll(live, offset, axis=1)
        row_sums, col_sums = lax.map(cross_tile, (flatten(blocks), flatten(live), flatten(moved_blocks), flatten(moved_live)))
        density = density + row_sums.reshape(N_GEN, N_JOIN, BLOCK)
        density = density + jnp.roll(col_sums.reshape(N_GEN, N_JOIN, BLOCK), -offset, axis=1)
    weight = live / (density + 1.0 - live)
    return weight.reshape(ROWS)
```

```python
import math

import jax
import jax.numpy as jnp
from jax import lax
from jax.experimental import pallas as pl
from jax.experimental.pallas import tpu as pltpu
from jax.sharding import PartitionSpec as P

ROUNDS = 3
MESH = pl.DeviceIdType.MESH
SCALE = 8.0 * math.log2(math.e)
LAYERS = 4
OWN, SIB, XN, XS, YN = range(5)


def shifted(block, axis, distance):
    devices = range(lax.axis_size(axis))
    route = [((i - distance) % len(devices), i) for i in devices]
    return lax.ppermute(block, axis, route)


def tile_sums(left_rows, left_live, right_rows, right_live):
    row_count = left_rows.shape[0]
    piece_rows = min(512, row_count)
    pieces = row_count // piece_rows

    def one_piece(col_total, operands):
        piece_block, piece_live = operands
        scores = lax.dot_general(
            piece_block, right_rows, (((1,), (1,)), ((), ())), preferred_element_type=jnp.float32
        )
        kernel = jnp.exp(8.0 * (scores - 1.0))
        return (
            col_total + jnp.sum(kernel * piece_live[:, None], axis=0),
            jnp.sum(kernel * right_live[None, :], axis=1),
        )

    start_total = jnp.zeros((right_rows.shape[0],), jnp.float32)
    col_sums, row_sums = lax.scan(
        one_piece,
        start_total,
        (
            left_rows.reshape(pieces, piece_rows, left_rows.shape[1]),
            left_live.reshape(pieces, piece_rows),
        ),
    )
    return (row_sums.reshape(row_count), col_sums)


def ring_body(src_emb, counts):
    values = src_emb.astype(jnp.float32)
    width = values.shape[1]
    unit = (
        values
        * lax.rsqrt(jnp.mean(values * values, axis=1, keepdims=True) + 1e-06)
        / math.sqrt(width)
    ).astype(jnp.bfloat16)
    nodes = lax.axis_size(("gen", "join"))
    block_rows = unit.shape[0]
    slots = block_rows // nodes
    received, got_counts = (
        lax.all_to_all(
            unit.reshape(nodes, slots, width),
            ("gen", "join"),
            split_axis=0,
            concat_axis=0,
            tiled=True,
        ),
        lax.all_to_all(
            counts.reshape(nodes), ("gen", "join"), split_axis=0, concat_axis=0, tiled=True
        ),
    )
    owned = received.reshape(block_rows, width)
    slot_index = lax.broadcasted_iota(jnp.int32, (nodes, slots), 1)
    live = (slot_index < got_counts.reshape(nodes, 1)).astype(jnp.float32).reshape(block_rows)
    live_wire = live.astype(jnp.bfloat16)
    density = tile_sums(owned, live, owned, live)[0]
    for shift_by in range(1, ROUNDS + 1):
        other_rows, other_flags = shifted((owned, live_wire), "join", shift_by)
        row_sums, col_sums = tile_sums(owned, live, other_rows, other_flags.astype(jnp.float32))
        density = density + row_sums + shifted(col_sums, "join", -shift_by)
    return live / (density + 1.0 - live)


def layer_kernel(slots, width, src, counts, counts_row, out, held, snd, racc, dacc, cacc, msg, got,
                 live, zsend, zrecv, lsend, lrecv, csend, crecv, wsend, wrecv):
    gen, join = lax.axis_index("gen"), lax.axis_index("join")
    x, k, z, y = gen // 2, gen % 2, join // 2, join % 2
    inner = (z + 1) // 2 % 2
    outer = 1 - inner
    flip = z + 1 - 2 * (z % 2)
    over = (z + 2) % 4
    far = 3 - z
    owners = 8
    rows = owners * slots
    tall = 4 * slots
    pieces = LAYERS * owners
    order = [z, flip, outer * over + inner * far, outer * far + inner * over]
    sends = [
        (outer * flip + inner * far, outer + 2 * inner),
        (outer * over + inner * flip, 3 * outer + inner),
        (outer * far + inner * over, 3 * outer + 2 * inner),
    ]
    sibling = (2 * x + 1 - k, join)
    x_near = (2 * (1 - x) + k, join)
    y_near = (gen, 2 * z + 1 - y)

    barrier = pltpu.get_barrier_semaphore()
    for peer in (
        (gen, 2 * flip + y), (gen, 2 * over + y), (gen, 2 * far + y), x_near, y_near, sibling
    ):
        pl.semaphore_signal(barrier, inc=1, device_id=peer, device_id_type=MESH)
    elsewhere = ((gen - z) * (gen - z) + 8) // 9

    def greet(i, carry):
        @pl.when((i // 2) * owners + 2 * gen + i % 2 != gen * owners + join)
        def _():
            pl.semaphore_signal(
                barrier, inc=1, device_id=(i // 2, 2 * gen + i % 2), device_id_type=MESH
            )

        return carry

    lax.fori_loop(0, owners, greet, 0)

    def normalize(layer, b, into):
        start = pl.multiple_of(layer * rows + b * slots, slots)
        values = src[pl.ds(start, slots), :].astype(jnp.float32)
        spare = (counts[0, layer * owners + b]
                 - lax.broadcasted_iota(jnp.int32, (slots, 1), 0)).astype(jnp.float32)
        alive = jnp.clip(spare, 0.0, 1.0)
        factor = lax.rsqrt(jnp.mean(values * values, axis=1, keepdims=True) + 1e-06)
        into[...] = (values * (factor * (alive / math.sqrt(width)))).astype(jnp.bfloat16)

    def z_copy(slot, b):
        layer, place = sends[slot]
        return pltpu.make_async_remote_copy(
            src_ref=snd.at[slot, b], dst_ref=held.at[place, b, OWN],
            send_sem=zsend.at[slot], recv_sem=zrecv.at[place * owners + b],
            device_id=(gen, 2 * layer + y), device_id_type=MESH,
        )

    def c_copy(slot):
        layer, place = sends[slot]
        return pltpu.make_async_remote_copy(
            src_ref=live.at[0], dst_ref=live.at[place], send_sem=csend.at[slot],
            recv_sem=crecv.at[place], device_id=(gen, 2 * layer + y), device_id_type=MESH,
        )

    def l_copy(t, kind):
        d, b = t // owners, t % owners
        source = XN if kind == XS else OWN
        target = {SIB: sibling, XS: sibling, XN: x_near, YN: y_near}[kind]
        return pltpu.make_async_remote_copy(
            src_ref=held.at[d, b, source], dst_ref=held.at[d, b, kind],
            send_sem=lsend.at[(kind - 1) * LAYERS + d],
            recv_sem=lrecv.at[(kind - 1) * pieces + t],
            device_id=target, device_id_type=MESH,
        )

    def spread(t):
        for kind in (XN, YN, SIB):
            l_copy(t, kind).start()

    def arrive(t):
        d, b = t // owners, t % owners
        pltpu.make_async_remote_copy(
            src_ref=snd.at[0, 0], dst_ref=held.at[d, b, OWN],
            send_sem=zsend.at[0], recv_sem=zrecv.at[t],
            device_id=y_near, device_id_type=MESH,
        ).wait_recv()
        spread(t)

    def relay(t):
        l_copy(t, XN).wait_recv()
        l_copy(t, XS).start()

    def normalize_slot(slot):
        def one(b, carry):
            normalize(sends[slot][0], b, snd.at[slot, b])
            return carry

        lax.fori_loop(0, owners, one, 0)

    def send_slot(slot):
        def one(b, carry):
            z_copy(slot, b).start()
            return carry

        lax.fori_loop(0, owners, one, 0)

    def own_piece(b, carry):
        normalize(z, b, held.at[0, b, OWN])
        return carry

    normalize_slot(0)
    lax.fori_loop(0, owners, own_piece, 0)
    live[0] = jnp.zeros((8, 128), jnp.int32)
    live[0, 0:1, 0:32] = counts_row[...]
    pl.semaphore_wait(barrier, 13 + elsewhere)

    def first(b, carry):
        z_copy(0, b).start()
        spread(b)
        return carry

    lax.fori_loop(0, owners, first, 0)
    for slot in (1, 2):
        normalize_slot(slot)
        send_slot(slot)
    for slot in range(3):
        c_copy(slot).start()
    racc[...] = jnp.zeros_like(racc)
    dacc[...] = jnp.zeros_like(dacc)

    lane_owner = lax.broadcasted_iota(jnp.int32, (1, rows), 1) // slots
    ones = jnp.ones((16, 128), jnp.bfloat16)

    def reduce_columns(t):
        sums = cacc[t % 2]
        high = sums.astype(jnp.bfloat16)
        low = (sums - high.astype(jnp.float32)).astype(jnp.bfloat16)
        flat = (((1,), (1,)), ((), ()))
        line = lax.dot_general(ones, high, flat, preferred_element_type=jnp.float32)
        line += lax.dot_general(ones, low, flat, preferred_element_type=jnp.float32)
        msg[t % owners, pl.ds(t // owners, 1), 0:tall] = line[0:1, :]

    def kernel_of(left, right):
        scores = lax.dot_general(
            left, right, (((1,), (1,)), ((), ())), preferred_element_type=jnp.float32
        )
        return jnp.exp2(scores * SCALE)

    def down(values):
        return jnp.sum(values.reshape(values.shape[0] // 8, 8, values.shape[1]), axis=0)

    def across(values):
        total = values[:, 0:128]
        for c in range(1, values.shape[1] // 128):
            total = total + values[:, 128 * c:128 * (c + 1)]
        return total

    def tile(d, b):
        left = held[d, b, 0:4].reshape(tall, width)
        near = jnp.where(lane_owner != (b + 4) % owners, 1.0, 0.0)
        total = None
        for i in range(d):
            for r, kind in enumerate((OWN, YN)):
                kernel = kernel_of(left, held[i, :, kind].reshape(rows, width)) * near
                racc[r, i] += down(kernel)
                part = across(kernel)
                total = part if total is None else total + part
        picks = []
        for m in (0, 1, 2, 3, 5, 6, 7):
            valid = (b - m + owners) // owners
            picks.append((m, valid, (b - m) * valid))
        picks = [(r, kind) + pick for r, kind in enumerate((OWN, YN)) for pick in picks]
        right = jnp.concatenate([held[d, a, kind] for r, kind, m, valid, a in picks], axis=0)
        kernel = kernel_of(left, right)
        lanes = lax.broadcasted_iota(jnp.int32, (1, len(picks) * slots), 1) // slots
        use = jnp.zeros((1, len(picks) * slots), jnp.float32)
        for n, (r, kind, m, valid, a) in enumerate(picks):
            if m:
                use = jnp.where(lanes == n, valid.astype(jnp.float32), use)
        part = across(kernel * use)
        sums = down(kernel)
        for n, (r, kind, m, valid, a) in enumerate(picks):
            piece = sums[:, n * slots:(n + 1) * slots]
            if m:
                piece = piece * valid.astype(jnp.float32)
            dacc[r, d, a, :, 0:slots] += piece
        cacc[(d * owners + b) % 2] = part if total is None else total + part

    relay(0)
    for d in range(LAYERS):
        def step(b, carry):
            t = d * owners + b

            @pl.when((t + 4 < pieces) & (t + 4 >= owners))
            def _():
                arrive(t + 4)

            @pl.when(t + 1 < pieces)
            def _():
                relay(t + 1)

            for kind in (SIB, YN, XS):
                l_copy(t, kind).wait_recv()
            @pl.when(t > 0)
            def _():
                reduce_columns(t - 1)
            tile(d, b)
            return carry

        lax.fori_loop(0, owners, step, 0)
        if d == 1:
            for place in range(1, LAYERS):
                pltpu.make_async_remote_copy(
                    src_ref=live.at[0], dst_ref=live.at[place], send_sem=csend.at[0],
                    recv_sem=crecv.at[place], device_id=y_near, device_id_type=MESH,
                ).wait_recv()
            lane = lax.broadcasted_iota(jnp.int32, (owners, 128), 1)
            mine = owners * z + lax.broadcasted_iota(jnp.int32, (owners, 128), 0)
            across_of = owners * z + (4 + lax.broadcasted_iota(jnp.int32, (owners, 128), 0)) % owners
            group = (lane >= owners * z) & (lane < owners * z + owners) & (lane != across_of)
            slot_index = lax.broadcasted_iota(jnp.int32, (owners, slots), 1).astype(jnp.float32)
            dead = jnp.zeros((owners, 128), jnp.float32)
            for place in range(LAYERS):
                filled = jnp.broadcast_to(live[place, 0:1, :].astype(jnp.float32), (owners, 128))
                limit = jnp.sum(jnp.where(lane == mine, filled, 0.0), axis=1, keepdims=True)
                flags = jnp.where(slot_index < limit, 1.0, 0.0)
                for j in range(owners):
                    msg[j, place:place + 1, 6 * slots:7 * slots] = flags[j:j + 1, :]
                dead = dead + jnp.where(group, float(slots) - filled, 0.0)
            missing = jnp.broadcast_to(jnp.sum(dead, axis=1, keepdims=True), (owners, slots))
            for j in range(owners):
                msg[j, 0:1, 7 * slots:8 * slots] = missing[j:j + 1, :]

    reduce_columns(pieces - 1)
    for r in range(2):
        for d in range(LAYERS):
            line = jnp.sum(racc[r, d], axis=0, keepdims=True)
            for j in range(owners):
                extra = jnp.sum(dacc[r, d, j, :, 0:slots], axis=0, keepdims=True)
                msg[j, d:d + 1, (4 + r) * slots:(5 + r) * slots] = (
                    line[:, j * slots:(j + 1) * slots] + extra
                )

    spot = 2 * gen + y

    def w_copy(j):
        return pltpu.make_async_remote_copy(
            src_ref=msg.at[j], dst_ref=got.at[spot], send_sem=wsend.at[j],
            recv_sem=wrecv.at[spot], device_id=(z, j), device_id_type=MESH,
        )

    def send(j, carry):
        @pl.when(z * owners + j != gen * owners + join)
        def _():
            w_copy(j).start()

        @pl.when(z * owners + j == gen * owners + join)
        def _():
            got[spot] = msg[j]

        return carry

    lax.fori_loop(0, owners, send, 0)

    def receive(i, carry):
        @pl.when((i // 2) * owners + 2 * gen + i % 2 != gen * owners + join)
        def _():
            pltpu.make_async_remote_copy(
                src_ref=msg.at[0], dst_ref=got.at[i], send_sem=wsend.at[0],
                recv_sem=wrecv.at[i], device_id=y_near, device_id_type=MESH,
            ).wait_recv()

        return carry

    lax.fori_loop(0, owners, receive, 0)

    missing = got[0, 0:1, 7 * slots:8 * slots]
    for q in range(1, owners):
        missing = missing + got[q, 0:1, 7 * slots:8 * slots]
    g_inner = (gen + 1) // 2 % 2
    g_outer = 1 - g_inner
    g_over, g_far = (gen + 2) % 4, 3 - gen
    g_order = [
        gen, gen + 1 - 2 * (gen % 2), g_outer * g_over + g_inner * g_far,
        g_outer * g_far + g_inner * g_over,
    ]
    for pair in range(4):
        halves = []
        for half in range(2):
            q = 2 * pair + half

            def field(sender, n):
                return got[sender, 0:LAYERS, n * slots:(n + 1) * slots]

            total = field(q, 0) + field(q ^ 2, 1) + field(q ^ 4, 2) + field(q ^ 6, 3)
            total = total + field(q, 4) + field(q ^ 1, 5)
            flags = field(q, 6)
            density = (total - missing) * math.exp(-8.0)
            halves.append(flags / (density + 1.0 - flags))
        both = jnp.concatenate(halves, axis=1)
        for d in range(LAYERS):
            out[pl.ds(LAYERS * pair + g_order[d], 1), :] = both[d:d + 1, :]

    def sent(j, carry):
        @pl.when(z * owners + j != gen * owners + join)
        def _():
            w_copy(j).wait_send()

        return carry

    lax.fori_loop(0, owners, sent, 0)
    for slot in range(3):
        c_copy(slot).wait_send()
        pltpu.make_async_remote_copy(
            src_ref=snd.at[slot], dst_ref=snd.at[slot], send_sem=zsend.at[slot],
            recv_sem=zrecv.at[0], device_id=y_near, device_id_type=MESH,
        ).wait_send()
    for d in range(LAYERS):
        for kind in (SIB, XN, XS, YN):
            pltpu.make_async_remote_copy(
                src_ref=held.at[d, :, kind], dst_ref=held.at[d, :, kind],
                send_sem=lsend.at[(kind - 1) * LAYERS + d],
                recv_sem=lrecv.at[0], device_id=y_near, device_id_type=MESH,
            ).wait_send()


def layer_body(src_emb, counts):
    block, width = src_emb.shape
    owners = 8
    slots = block // (LAYERS * owners)
    vmem = pl.BlockSpec(memory_space=pltpu.VMEM)
    weights = pl.pallas_call(
        lambda *refs: layer_kernel(slots, width, *refs),
        out_shape=jax.ShapeDtypeStruct((block // 128, 128), jnp.float32),
        in_specs=[vmem, pl.BlockSpec(memory_space=pltpu.SMEM), vmem],
        out_specs=vmem,
        scratch_shapes=[
            pltpu.VMEM((LAYERS, owners, 5, slots, width), jnp.bfloat16),
            pltpu.VMEM((LAYERS - 1, owners, slots, width), jnp.bfloat16),
            pltpu.VMEM((2, LAYERS, 8, owners * slots), jnp.float32),
            pltpu.VMEM((2, LAYERS, owners, 8, 128), jnp.float32),
            pltpu.VMEM((2, 4 * slots, 128), jnp.float32),
            pltpu.VMEM((owners, 8, 8 * slots), jnp.float32),
            pltpu.VMEM((owners, 8, 8 * slots), jnp.float32),
            pltpu.VMEM((LAYERS, 8, 128), jnp.int32),
            pltpu.SemaphoreType.DMA((3,)),
            pltpu.SemaphoreType.DMA((LAYERS * owners,)),
            pltpu.SemaphoreType.DMA((4 * LAYERS,)),
            pltpu.SemaphoreType.DMA((4 * LAYERS * owners,)),
            pltpu.SemaphoreType.DMA((3,)),
            pltpu.SemaphoreType.DMA((LAYERS,)),
            pltpu.SemaphoreType.DMA((owners,)),
            pltpu.SemaphoreType.DMA((owners,)),
        ],
        compiler_params=pltpu.CompilerParams(
            collective_id=0, has_side_effects=True, vmem_limit_bytes=56 * 2**20
        ),
        name="layer_kernel",
    )(src_emb, counts, counts)
    return weights.reshape(block)


def solution(mesh):
    in_specs = (P(("gen", "join"), None), P(("gen", "join"), None))
    out_specs = P(("gen", "join"))
    fits = mesh.shape["gen"] == 4 and mesh.shape["join"] == 8
    body = layer_body if fits else ring_body
    return jax.shard_map(body, mesh=mesh, in_specs=in_specs, out_specs=out_specs, check_vma=False)
```

```python
import math

import jax
import jax.numpy as jnp
from jax import lax
from jax.experimental import pallas as pl
from jax.experimental.pallas import tpu as pltpu
from jax.sharding import PartitionSpec as P

ROUNDS = 3
MESH = pl.DeviceIdType.MESH
SCALE = 8.0 * math.log2(math.e)
LAYERS = 4
OWN, SIB, XN, XS, YN = range(5)


def shifted(block, axis, distance):
    devices = range(lax.axis_size(axis))
    route = [((i - distance) % len(devices), i) for i in devices]
    return lax.ppermute(block, axis, route)


def tile_sums(left_rows, left_live, right_rows, right_live):
    row_count = left_rows.shape[0]
    piece_rows = min(512, row_count)
    pieces = row_count // piece_rows

    def one_piece(col_total, operands):
        piece_block, piece_live = operands
        scores = lax.dot_general(
            piece_block, right_rows, (((1,), (1,)), ((), ())), preferred_element_type=jnp.float32
        )
        kernel = jnp.exp(8.0 * (scores - 1.0))
        return (
            col_total + jnp.sum(kernel * piece_live[:, None], axis=0),
            jnp.sum(kernel * right_live[None, :], axis=1),
        )

    start_total = jnp.zeros((right_rows.shape[0],), jnp.float32)
    col_sums, row_sums = lax.scan(
        one_piece,
        start_total,
        (
            left_rows.reshape(pieces, piece_rows, left_rows.shape[1]),
            left_live.reshape(pieces, piece_rows),
        ),
    )
    return (row_sums.reshape(row_count), col_sums)


def ring_body(src_emb, counts):
    values = src_emb.astype(jnp.float32)
    width = values.shape[1]
    unit = (
        values
        * lax.rsqrt(jnp.mean(values * values, axis=1, keepdims=True) + 1e-06)
        / math.sqrt(width)
    ).astype(jnp.bfloat16)
    nodes = lax.axis_size(("gen", "join"))
    block_rows = unit.shape[0]
    slots = block_rows // nodes
    received, got_counts = (
        lax.all_to_all(
            unit.reshape(nodes, slots, width),
            ("gen", "join"),
            split_axis=0,
            concat_axis=0,
            tiled=True,
        ),
        lax.all_to_all(
            counts.reshape(nodes), ("gen", "join"), split_axis=0, concat_axis=0, tiled=True
        ),
    )
    owned = received.reshape(block_rows, width)
    slot_index = lax.broadcasted_iota(jnp.int32, (nodes, slots), 1)
    live = (slot_index < got_counts.reshape(nodes, 1)).astype(jnp.float32).reshape(block_rows)
    live_wire = live.astype(jnp.bfloat16)
    density = tile_sums(owned, live, owned, live)[0]
    for shift_by in range(1, ROUNDS + 1):
        other_rows, other_flags = shifted((owned, live_wire), "join", shift_by)
        row_sums, col_sums = tile_sums(owned, live, other_rows, other_flags.astype(jnp.float32))
        density = density + row_sums + shifted(col_sums, "join", -shift_by)
    return live / (density + 1.0 - live)


def layer_kernel(slots, width, src, counts, counts_row, out, held, snd, racc, dacc, cacc, msg, got,
                 live, zsend, zrecv, lsend, lrecv, csend, crecv, wsend, wrecv):
    gen, join = lax.axis_index("gen"), lax.axis_index("join")
    x, k, z, y = gen // 2, gen % 2, join // 2, join % 2
    inner = (z + 1) // 2 % 2
    flip = z + 1 - 2 * (z % 2)
    over = (z + 2) % 4
    far = 3 - z
    owners = 8
    rows = owners * slots
    tall = 4 * slots
    pieces = LAYERS * owners
    peers = [flip, far, over]
    sibling = (2 * x + 1 - k, join)
    x_near = (2 * (1 - x) + k, join)
    y_near = (gen, 2 * z + 1 - y)

    barrier = pltpu.get_barrier_semaphore()
    for peer in (
        (gen, 2 * flip + y), (gen, 2 * over + y), (gen, 2 * far + y), x_near, y_near, sibling
    ):
        pl.semaphore_signal(barrier, inc=1, device_id=peer, device_id_type=MESH)
    elsewhere = ((gen - z) * (gen - z) + 8) // 9

    def greet(i, carry):
        @pl.when((i // 2) * owners + 2 * gen + i % 2 != gen * owners + join)
        def _():
            pl.semaphore_signal(
                barrier, inc=1, device_id=(i // 2, 2 * gen + i % 2), device_id_type=MESH
            )

        return carry

    lax.fori_loop(0, owners, greet, 0)

    def normalize(layer, b, into):
        start = pl.multiple_of(layer * rows + b * slots, slots)
        values = src[pl.ds(start, slots), :].astype(jnp.float32)
        spare = (counts[0, layer * owners + b]
                 - lax.broadcasted_iota(jnp.int32, (slots, 1), 0)).astype(jnp.float32)
        alive = jnp.clip(spare, 0.0, 1.0)
        factor = lax.rsqrt(jnp.mean(values * values, axis=1, keepdims=True) + 1e-06)
        into[...] = (values * (factor * (alive / math.sqrt(width)))).astype(jnp.bfloat16)

    def z_copy(slot, b):
        return pltpu.make_async_remote_copy(
            src_ref=snd.at[slot, b], dst_ref=held.at[slot + 1, b, OWN],
            send_sem=zsend.at[slot], recv_sem=zrecv.at[(slot + 1) * owners + b],
            device_id=(gen, 2 * peers[slot] + y), device_id_type=MESH,
        )

    def c_copy(slot):
        return pltpu.make_async_remote_copy(
            src_ref=live.at[0], dst_ref=live.at[slot + 1], send_sem=csend.at[slot],
            recv_sem=crecv.at[slot + 1], device_id=(gen, 2 * peers[slot] + y),
            device_id_type=MESH,
        )

    def l_copy(t, kind):
        d, b = t // owners, t % owners
        source = XN if kind == XS else OWN
        target = {SIB: sibling, XS: sibling, XN: x_near, YN: y_near}[kind]
        return pltpu.make_async_remote_copy(
            src_ref=held.at[d, b, source], dst_ref=held.at[d, b, kind],
            send_sem=lsend.at[(kind - 1) * LAYERS + d],
            recv_sem=lrecv.at[(kind - 1) * pieces + t],
            device_id=target, device_id_type=MESH,
        )

    def spread(t):
        for kind in (XN, YN, SIB):
            l_copy(t, kind).start()

    def arrive(t):
        d, b = t // owners, t % owners
        pltpu.make_async_remote_copy(
            src_ref=snd.at[0, 0], dst_ref=held.at[d, b, OWN],
            send_sem=zsend.at[0], recv_sem=zrecv.at[t],
            device_id=y_near, device_id_type=MESH,
        ).wait_recv()
        spread(t)

    def relay(t):
        l_copy(t, XN).wait_recv()
        l_copy(t, XS).start()

    def normalize_slot(slot):
        def one(b, carry):
            normalize(peers[slot], b, snd.at[slot, b])
            return carry

        lax.fori_loop(0, owners, one, 0)

    def own_piece(b, carry):
        normalize(z, b, held.at[0, b, OWN])
        return carry

    lax.fori_loop(0, owners, own_piece, 0)
    normalize_slot(0)
    normalize_slot(1)
    live[0] = jnp.zeros((8, 128), jnp.int32)
    live[0, 0:1, 0:32] = counts_row[...]
    pl.semaphore_wait(barrier, 13 + elsewhere)

    for slot in range(3):
        c_copy(slot).start()

    def first(b, carry):
        @pl.when(inner == 1)
        def _():
            z_copy(1, b).start()

        z_copy(0, b).start()
        spread(b)
        return carry

    lax.fori_loop(0, owners, first, 0)
    normalize_slot(2)

    def second(b, carry):
        @pl.when(inner == 0)
        def _():
            z_copy(1, b).start()

        z_copy(2, b).start()
        return carry

    lax.fori_loop(0, owners, second, 0)
    racc[...] = jnp.zeros_like(racc)
    dacc[...] = jnp.zeros_like(dacc)

    lane_owner = lax.broadcasted_iota(jnp.int32, (1, rows), 1) // slots
    ones = jnp.ones((16, 128), jnp.bfloat16)

    def reduce_columns(t):
        sums = cacc[t % 2]
        high = sums.astype(jnp.bfloat16)
        low = (sums - high.astype(jnp.float32)).astype(jnp.bfloat16)
        flat = (((1,), (1,)), ((), ()))
        line = lax.dot_general(ones, high, flat, preferred_element_type=jnp.float32)
        line += lax.dot_general(ones, low, flat, preferred_element_type=jnp.float32)
        msg[t % owners, pl.ds(t // owners, 1), 0:tall] = line[0:1, :]

    def kernel_of(left, right):
        scores = lax.dot_general(
            left, right, (((1,), (1,)), ((), ())), preferred_element_type=jnp.float32
        )
        return jnp.exp2(scores * SCALE)

    def down(values):
        return jnp.sum(values.reshape(values.shape[0] // 8, 8, values.shape[1]), axis=0)

    def across(values):
        total = values[:, 0:128]
        for c in range(1, values.shape[1] // 128):
            total = total + values[:, 128 * c:128 * (c + 1)]
        return total

    def tile(d, b):
        left = held[d, b, 0:4].reshape(tall, width)
        near = jnp.where(lane_owner != (b + 4) % owners, 1.0, 0.0)
        total = None
        for i in range(d):
            for r, kind in enumerate((OWN, YN)):
                kernel = kernel_of(left, held[i, :, kind].reshape(rows, width)) * near
                racc[r, i] += down(kernel)
                part = across(kernel)
                total = part if total is None else total + part
        picks = []
        for m in (0, 1, 2, 3, 5, 6, 7):
            valid = (b - m + owners) // owners
            picks.append((m, valid, (b - m) * valid))
        picks = [(r, kind) + pick for r, kind in enumerate((OWN, YN)) for pick in picks]
        right = jnp.concatenate([held[d, a, kind] for r, kind, m, valid, a in picks], axis=0)
        kernel = kernel_of(left, right)
        lanes = lax.broadcasted_iota(jnp.int32, (1, len(picks) * slots), 1) // slots
        use = jnp.zeros((1, len(picks) * slots), jnp.float32)
        for n, (r, kind, m, valid, a) in enumerate(picks):
            if m:
                use = jnp.where(lanes == n, valid.astype(jnp.float32), use)
        part = across(kernel * use)
        sums = down(kernel)
        for n, (r, kind, m, valid, a) in enumerate(picks):
            piece = sums[:, n * slots:(n + 1) * slots]
            if m:
                piece = piece * valid.astype(jnp.float32)
            dacc[r, d, a, :, 0:slots] += piece
        cacc[(d * owners + b) % 2] = part if total is None else total + part

    relay(0)
    for d in range(LAYERS):
        def step(b, carry):
            t = d * owners + b

            @pl.when((t + 4 < pieces) & (t + 4 >= owners))
            def _():
                arrive(t + 4)

            @pl.when(t + 1 < pieces)
            def _():
                relay(t + 1)

            for kind in (SIB, YN, XS):
                l_copy(t, kind).wait_recv()
            @pl.when(t > 0)
            def _():
                reduce_columns(t - 1)
            tile(d, b)
            return carry

        lax.fori_loop(0, owners, step, 0)
        if d == 1:
            for place in range(1, LAYERS):
                pltpu.make_async_remote_copy(
                    src_ref=live.at[0], dst_ref=live.at[place], send_sem=csend.at[0],
                    recv_sem=crecv.at[place], device_id=y_near, device_id_type=MESH,
                ).wait_recv()
            lane = lax.broadcasted_iota(jnp.int32, (owners, 128), 1)
            mine = owners * z + lax.broadcasted_iota(jnp.int32, (owners, 128), 0)
            across_of = owners * z + (4 + lax.broadcasted_iota(jnp.int32, (owners, 128), 0)) % owners
            group = (lane >= owners * z) & (lane < owners * z + owners) & (lane != across_of)
            slot_index = lax.broadcasted_iota(jnp.int32, (owners, slots), 1).astype(jnp.float32)
            dead = jnp.zeros((owners, 128), jnp.float32)
            for place in range(LAYERS):
                filled = jnp.broadcast_to(live[place, 0:1, :].astype(jnp.float32), (owners, 128))
                limit = jnp.sum(jnp.where(lane == mine, filled, 0.0), axis=1, keepdims=True)
                flags = jnp.where(slot_index < limit, 1.0, 0.0)
                for j in range(owners):
                    msg[j, place:place + 1, 6 * slots:7 * slots] = flags[j:j + 1, :]
                dead = dead + jnp.where(group, float(slots) - filled, 0.0)
            missing = jnp.broadcast_to(jnp.sum(dead, axis=1, keepdims=True), (owners, slots))
            for j in range(owners):
                msg[j, 0:1, 7 * slots:8 * slots] = missing[j:j + 1, :]

    reduce_columns(pieces - 1)
    for r in range(2):
        for d in range(LAYERS):
            line = jnp.sum(racc[r, d], axis=0, keepdims=True)
            for j in range(owners):
                extra = jnp.sum(dacc[r, d, j, :, 0:slots], axis=0, keepdims=True)
                msg[j, d:d + 1, (4 + r) * slots:(5 + r) * slots] = (
                    line[:, j * slots:(j + 1) * slots] + extra
                )

    spot = 2 * gen + y

    def w_copy(j):
        return pltpu.make_async_remote_copy(
            src_ref=msg.at[j], dst_ref=got.at[spot], send_sem=wsend.at[j],
            recv_sem=wrecv.at[spot], device_id=(z, j), device_id_type=MESH,
        )

    def send(j, carry):
        @pl.when(z * owners + j != gen * owners + join)
        def _():
            w_copy(j).start()

        @pl.when(z * owners + j == gen * owners + join)
        def _():
            got[spot] = msg[j]

        return carry

    lax.fori_loop(0, owners, send, 0)

    def receive(i, carry):
        @pl.when((i // 2) * owners + 2 * gen + i % 2 != gen * owners + join)
        def _():
            pltpu.make_async_remote_copy(
                src_ref=msg.at[0], dst_ref=got.at[i], send_sem=wsend.at[0],
                recv_sem=wrecv.at[i], device_id=y_near, device_id_type=MESH,
            ).wait_recv()

        return carry

    lax.fori_loop(0, owners, receive, 0)

    missing = got[0, 0:1, 7 * slots:8 * slots]
    for q in range(1, owners):
        missing = missing + got[q, 0:1, 7 * slots:8 * slots]
    g_order = [gen, gen + 1 - 2 * (gen % 2), 3 - gen, (gen + 2) % 4]
    for pair in range(4):
        halves = []
        for half in range(2):
            q = 2 * pair + half

            def field(sender, n):
                return got[sender, 0:LAYERS, n * slots:(n + 1) * slots]

            total = field(q, 0) + field(q ^ 2, 1) + field(q ^ 4, 2) + field(q ^ 6, 3)
            total = total + field(q, 4) + field(q ^ 1, 5)
            flags = field(q, 6)
            density = (total - missing) * math.exp(-8.0)
            halves.append(flags / (density + 1.0 - flags))
        both = jnp.concatenate(halves, axis=1)
        for d in range(LAYERS):
            out[pl.ds(LAYERS * pair + g_order[d], 1), :] = both[d:d + 1, :]

    def sent(j, carry):
        @pl.when(z * owners + j != gen * owners + join)
        def _():
            w_copy(j).wait_send()

        return carry

    lax.fori_loop(0, owners, sent, 0)
    for slot in range(3):
        c_copy(slot).wait_send()
        pltpu.make_async_remote_copy(
            src_ref=snd.at[slot], dst_ref=snd.at[slot], send_sem=zsend.at[slot],
            recv_sem=zrecv.at[0], device_id=y_near, device_id_type=MESH,
        ).wait_send()
    for d in range(LAYERS):
        for kind in (SIB, XN, XS, YN):
            pltpu.make_async_remote_copy(
                src_ref=held.at[d, :, kind], dst_ref=held.at[d, :, kind],
                send_sem=lsend.at[(kind - 1) * LAYERS + d],
                recv_sem=lrecv.at[0], device_id=y_near, device_id_type=MESH,
            ).wait_send()


def layer_body(src_emb, counts):
    block, width = src_emb.shape
    owners = 8
    slots = block // (LAYERS * owners)
    vmem = pl.BlockSpec(memory_space=pltpu.VMEM)
    weights = pl.pallas_call(
        lambda *refs: layer_kernel(slots, width, *refs),
        out_shape=jax.ShapeDtypeStruct((block // 128, 128), jnp.float32),
        in_specs=[vmem, pl.BlockSpec(memory_space=pltpu.SMEM), vmem],
        out_specs=vmem,
        scratch_shapes=[
            pltpu.VMEM((LAYERS, owners, 5, slots, width), jnp.bfloat16),
            pltpu.VMEM((LAYERS - 1, owners, slots, width), jnp.bfloat16),
            pltpu.VMEM((2, LAYERS, 8, owners * slots), jnp.float32),
            pltpu.VMEM((2, LAYERS, owners, 8, 128), jnp.float32),
            pltpu.VMEM((2, 4 * slots, 128), jnp.float32),
            pltpu.VMEM((owners, 8, 8 * slots), jnp.float32),
            pltpu.VMEM((owners, 8, 8 * slots), jnp.float32),
            pltpu.VMEM((LAYERS, 8, 128), jnp.int32),
            pltpu.SemaphoreType.DMA((3,)),
            pltpu.SemaphoreType.DMA((LAYERS * owners,)),
            pltpu.SemaphoreType.DMA((4 * LAYERS,)),
            pltpu.SemaphoreType.DMA((4 * LAYERS * owners,)),
            pltpu.SemaphoreType.DMA((3,)),
            pltpu.SemaphoreType.DMA((LAYERS,)),
            pltpu.SemaphoreType.DMA((owners,)),
            pltpu.SemaphoreType.DMA((owners,)),
        ],
        compiler_params=pltpu.CompilerParams(
            collective_id=0, has_side_effects=True, vmem_limit_bytes=56 * 2**20
        ),
        name="layer_kernel",
    )(src_emb, counts, counts)
    return weights.reshape(block)


def solution(mesh):
    in_specs = (P(("gen", "join"), None), P(("gen", "join"), None))
    out_specs = P(("gen", "join"))
    fits = mesh.shape["gen"] == 4 and mesh.shape["join"] == 8
    body = layer_body if fits else ring_body
    return jax.shard_map(body, mesh=mesh, in_specs=in_specs, out_specs=out_specs, check_vma=False)
```

```python
import math

import jax
import jax.numpy as jnp
from jax import lax
from jax.experimental import pallas as pl
from jax.experimental.pallas import tpu as pltpu
from jax.sharding import PartitionSpec as P

ROUNDS = 3
MESH = pl.DeviceIdType.MESH
SCALE = 8.0 * math.log2(math.e)
LAYERS = 4
OWN, SIB, XN, XS, YN = range(5)


def shifted(block, axis, distance):
    devices = range(lax.axis_size(axis))
    route = [((i - distance) % len(devices), i) for i in devices]
    return lax.ppermute(block, axis, route)


def tile_sums(left_rows, left_live, right_rows, right_live):
    row_count = left_rows.shape[0]
    piece_rows = min(512, row_count)
    pieces = row_count // piece_rows

    def one_piece(col_total, operands):
        piece_block, piece_live = operands
        scores = lax.dot_general(
            piece_block, right_rows, (((1,), (1,)), ((), ())), preferred_element_type=jnp.float32
        )
        kernel = jnp.exp(8.0 * (scores - 1.0))
        return (
            col_total + jnp.sum(kernel * piece_live[:, None], axis=0),
            jnp.sum(kernel * right_live[None, :], axis=1),
        )

    start_total = jnp.zeros((right_rows.shape[0],), jnp.float32)
    col_sums, row_sums = lax.scan(
        one_piece,
        start_total,
        (
            left_rows.reshape(pieces, piece_rows, left_rows.shape[1]),
            left_live.reshape(pieces, piece_rows),
        ),
    )
    return (row_sums.reshape(row_count), col_sums)


def ring_body(src_emb, counts):
    values = src_emb.astype(jnp.float32)
    width = values.shape[1]
    unit = (
        values
        * lax.rsqrt(jnp.mean(values * values, axis=1, keepdims=True) + 1e-06)
        / math.sqrt(width)
    ).astype(jnp.bfloat16)
    nodes = lax.axis_size(("gen", "join"))
    block_rows = unit.shape[0]
    slots = block_rows // nodes
    received, got_counts = (
        lax.all_to_all(
            unit.reshape(nodes, slots, width),
            ("gen", "join"),
            split_axis=0,
            concat_axis=0,
            tiled=True,
        ),
        lax.all_to_all(
            counts.reshape(nodes), ("gen", "join"), split_axis=0, concat_axis=0, tiled=True
        ),
    )
    owned = received.reshape(block_rows, width)
    slot_index = lax.broadcasted_iota(jnp.int32, (nodes, slots), 1)
    live = (slot_index < got_counts.reshape(nodes, 1)).astype(jnp.float32).reshape(block_rows)
    live_wire = live.astype(jnp.bfloat16)
    density = tile_sums(owned, live, owned, live)[0]
    for shift_by in range(1, ROUNDS + 1):
        other_rows, other_flags = shifted((owned, live_wire), "join", shift_by)
        row_sums, col_sums = tile_sums(owned, live, other_rows, other_flags.astype(jnp.float32))
        density = density + row_sums + shifted(col_sums, "join", -shift_by)
    return live / (density + 1.0 - live)


def layer_kernel(slots, width, src_hbm, counts_hbm, out, src, counts, counts_row, held, snd, racc,
                 dacc, cacc, last, msg, got, live, insem, zsend, zrecv, lsend, lrecv, csend, crecv,
                 wsend, wrecv):
    gen, join = lax.axis_index("gen"), lax.axis_index("join")
    x, k, z, y = gen // 2, gen % 2, join // 2, join % 2
    inner = (z + 1) // 2 % 2
    flip = z + 1 - 2 * (z % 2)
    over = (z + 2) % 4
    far = 3 - z
    owners = 8
    rows = owners * slots
    tall = 4 * slots
    pieces = LAYERS * owners
    peers = [flip, far, over]
    sibling = (2 * x + 1 - k, join)
    x_near = (2 * (1 - x) + k, join)
    y_near = (gen, 2 * z + 1 - y)

    barrier = pltpu.get_barrier_semaphore()
    for peer in (
        (gen, 2 * flip + y), (gen, 2 * over + y), (gen, 2 * far + y), x_near, y_near, sibling
    ):
        pl.semaphore_signal(barrier, inc=1, device_id=peer, device_id_type=MESH)
    elsewhere = ((gen - z) * (gen - z) + 8) // 9

    def greet(i, carry):
        @pl.when((i // 2) * owners + 2 * gen + i % 2 != gen * owners + join)
        def _():
            pl.semaphore_signal(
                barrier, inc=1, device_id=(i // 2, 2 * gen + i % 2), device_id_type=MESH
            )

        return carry

    lax.fori_loop(0, owners, greet, 0)

    loads = [
        pltpu.make_async_copy(counts_hbm, counts, insem.at[LAYERS]),
        pltpu.make_async_copy(counts_hbm, counts_row, insem.at[LAYERS + 1]),
    ]
    for n, layer in enumerate([z] + peers):
        start = pl.multiple_of(layer * rows, rows)
        loads.append(
            pltpu.make_async_copy(src_hbm.at[pl.ds(start, rows)], src.at[n], insem.at[n])
        )
    for load in loads:
        load.start()

    def normalize(n, layer, b, into):
        start = pl.multiple_of(b * slots, slots)
        values = src[n, pl.ds(start, slots), :].astype(jnp.float32)
        spare = (counts[0, layer * owners + b]
                 - lax.broadcasted_iota(jnp.int32, (slots, 1), 0)).astype(jnp.float32)
        alive = jnp.clip(spare, 0.0, 1.0)
        factor = lax.rsqrt(jnp.mean(values * values, axis=1, keepdims=True) + 1e-06)
        into[...] = (values * (factor * (alive / math.sqrt(width)))).astype(jnp.bfloat16)

    def z_copy(slot, b):
        return pltpu.make_async_remote_copy(
            src_ref=snd.at[slot, b], dst_ref=held.at[slot + 1, b, OWN],
            send_sem=zsend.at[slot], recv_sem=zrecv.at[(slot + 1) * owners + b],
            device_id=(gen, 2 * peers[slot] + y), device_id_type=MESH,
        )

    def c_copy(slot):
        return pltpu.make_async_remote_copy(
            src_ref=live.at[0], dst_ref=live.at[slot + 1], send_sem=csend.at[slot],
            recv_sem=crecv.at[slot + 1], device_id=(gen, 2 * peers[slot] + y),
            device_id_type=MESH,
        )

    def l_copy(t, kind):
        d, b = t // owners, t % owners
        source = XN if kind == XS else OWN
        target = {SIB: sibling, XS: sibling, XN: x_near, YN: y_near}[kind]
        return pltpu.make_async_remote_copy(
            src_ref=held.at[d, b, source], dst_ref=held.at[d, b, kind],
            send_sem=lsend.at[(kind - 1) * LAYERS + d],
            recv_sem=lrecv.at[(kind - 1) * pieces + t],
            device_id=target, device_id_type=MESH,
        )

    def spread(t):
        for kind in (XN, YN, SIB):
            l_copy(t, kind).start()

    def arrive(t):
        d, b = t // owners, t % owners
        pltpu.make_async_remote_copy(
            src_ref=snd.at[0, 0], dst_ref=held.at[d, b, OWN],
            send_sem=zsend.at[0], recv_sem=zrecv.at[t],
            device_id=y_near, device_id_type=MESH,
        ).wait_recv()
        spread(t)

    def relay(t):
        l_copy(t, XN).wait_recv()
        l_copy(t, XS).start()

    def normalize_slot(slot):
        def one(b, carry):
            normalize(slot + 1, peers[slot], b, snd.at[slot, b])
            return carry

        loads[slot + 3].wait()
        lax.fori_loop(0, owners, one, 0)

    def own_piece(b, carry):
        normalize(0, z, b, held.at[0, b, OWN])
        return carry

    for load in loads[:3]:
        load.wait()
    lax.fori_loop(0, owners, own_piece, 0)
    normalize_slot(0)
    normalize_slot(1)
    live[0] = jnp.zeros((8, 128), jnp.int32)
    live[0, 0:1, 0:32] = counts_row[...]
    pl.semaphore_wait(barrier, 13 + elsewhere)

    for slot in range(3):
        c_copy(slot).start()

    def first(b, carry):
        @pl.when(inner == 1)
        def _():
            z_copy(1, b).start()

        z_copy(0, b).start()
        spread(b)
        return carry

    lax.fori_loop(0, owners, first, 0)
    normalize_slot(2)

    def second(b, carry):
        @pl.when(inner == 0)
        def _():
            z_copy(1, b).start()

        z_copy(2, b).start()
        return carry

    lax.fori_loop(0, owners, second, 0)
    racc[...] = jnp.zeros_like(racc)
    dacc[...] = jnp.zeros_like(dacc)

    lane_owner = lax.broadcasted_iota(jnp.int32, (1, rows), 1) // slots
    ones = jnp.ones((16, 128), jnp.bfloat16)

    turns = [(r, m) for r in range(2) for m in (0, 1, 2, 3, 5, 6, 7)]
    turn = lax.broadcasted_iota(jnp.int32, (1, len(turns) * slots), 1) // slots % 7
    turn = turn + turn // 4
    zero_one = jnp.minimum(turn, 1).astype(jnp.float32)

    def earlier(b, m):
        return (b - m) * ((b - m + owners) // owners)

    def settle(t):
        d, b = t // owners, t % owners
        sums = cacc[t % 2]
        high = sums.astype(jnp.bfloat16)
        low = (sums - high.astype(jnp.float32)).astype(jnp.bfloat16)
        flat = (((1,), (1,)), ((), ()))
        line = lax.dot_general(ones, high, flat, preferred_element_type=jnp.float32)
        line += lax.dot_general(ones, low, flat, preferred_element_type=jnp.float32)
        msg[b, pl.ds(d, 1), :] = line[0:1, :]
        for n, (r, m) in enumerate(turns):
            dacc[r, d, earlier(b, m), :, 0:slots] += last[t % 2, :, n * slots:(n + 1) * slots]

    def kernel_of(left, right):
        scores = lax.dot_general(
            left, right, (((1,), (1,)), ((), ())), preferred_element_type=jnp.float32
        )
        return jnp.exp2(scores * SCALE)

    def down(values):
        return jnp.sum(values.reshape(values.shape[0] // 8, 8, values.shape[1]), axis=0)

    def across(values):
        total = values[:, 0:128]
        for c in range(1, values.shape[1] // 128):
            total = total + values[:, 128 * c:128 * (c + 1)]
        return total

    def tile(d, b):
        left = held[d, b, 0:4].reshape(tall, width)
        right = jnp.concatenate(
            [held[d, earlier(b, m), (OWN, YN)[r]] for r, m in turns], axis=0
        )
        kernel = kernel_of(left, right)
        use = jnp.where(turn <= b, 1.0, 0.0)
        last[(d * owners + b) % 2] = down(kernel) * use
        total = across(kernel * (use * zero_one))
        near = jnp.where(lane_owner != (b + 4) % owners, 1.0, 0.0)
        for i in range(d):
            for r, kind in enumerate((OWN, YN)):
                kernel = kernel_of(left, held[i, :, kind].reshape(rows, width))
                racc[r, i] += down(kernel) * near
                total = total + across(kernel * near)
        cacc[(d * owners + b) % 2] = total

    relay(0)
    for d in range(LAYERS):
        def step(b, carry):
            t = d * owners + b

            @pl.when((t + 4 < pieces) & (t + 4 >= owners))
            def _():
                arrive(t + 4)

            @pl.when(t + 1 < pieces)
            def _():
                relay(t + 1)

            for kind in (SIB, YN, XS):
                l_copy(t, kind).wait_recv()
            if d == 0:
                @pl.when(t > 0)
                def _():
                    settle(t - 1)

            else:
                settle(t - 1)
            tile(d, b)
            return carry

        lax.fori_loop(0, owners, step, 0)
        if d == 1:
            for place in range(1, LAYERS):
                pltpu.make_async_remote_copy(
                    src_ref=live.at[0], dst_ref=live.at[place], send_sem=csend.at[0],
                    recv_sem=crecv.at[place], device_id=y_near, device_id_type=MESH,
                ).wait_recv()
            lane = lax.broadcasted_iota(jnp.int32, (owners, 128), 1)
            mine = owners * z + lax.broadcasted_iota(jnp.int32, (owners, 128), 0)
            across_of = owners * z + (4 + lax.broadcasted_iota(jnp.int32, (owners, 128), 0)) % owners
            group = (lane >= owners * z) & (lane < owners * z + owners) & (lane != across_of)
            slot_index = lax.broadcasted_iota(jnp.int32, (owners, slots), 1).astype(jnp.float32)
            dead = jnp.zeros((owners, 128), jnp.float32)
            for place in range(LAYERS):
                filled = jnp.broadcast_to(live[place, 0:1, :].astype(jnp.float32), (owners, 128))
                limit = jnp.sum(jnp.where(lane == mine, filled, 0.0), axis=1, keepdims=True)
                flags = jnp.where(slot_index < limit, 1.0, 0.0)
                for j in range(owners):
                    msg[j, 4 + place:5 + place, 2 * slots:3 * slots] = flags[j:j + 1, :]
                dead = dead + jnp.where(group, float(slots) - filled, 0.0)
            missing = jnp.broadcast_to(jnp.sum(dead, axis=1, keepdims=True), (owners, slots))
            for j in range(owners):
                msg[j, 4:5, 3 * slots:4 * slots] = missing[j:j + 1, :]

    settle(pieces - 1)
    for r in range(2):
        for d in range(LAYERS):
            line = jnp.sum(racc[r, d], axis=0, keepdims=True)
            for j in range(owners):
                extra = jnp.sum(dacc[r, d, j, :, 0:slots], axis=0, keepdims=True)
                msg[j, 4 + d:5 + d, r * slots:(1 + r) * slots] = (
                    line[:, j * slots:(j + 1) * slots] + extra
                )

    spot = 2 * gen + y

    def w_copy(j):
        return pltpu.make_async_remote_copy(
            src_ref=msg.at[j], dst_ref=got.at[spot], send_sem=wsend.at[j],
            recv_sem=wrecv.at[spot], device_id=(z, j), device_id_type=MESH,
        )

    def send(j, carry):
        @pl.when(z * owners + j != gen * owners + join)
        def _():
            w_copy(j).start()

        @pl.when(z * owners + j == gen * owners + join)
        def _():
            got[spot] = msg[j]

        return carry

    lax.fori_loop(0, owners, send, 0)

    def receive(i, carry):
        @pl.when((i // 2) * owners + 2 * gen + i % 2 != gen * owners + join)
        def _():
            pltpu.make_async_remote_copy(
                src_ref=msg.at[0], dst_ref=got.at[i], send_sem=wsend.at[0],
                recv_sem=wrecv.at[i], device_id=y_near, device_id_type=MESH,
            ).wait_recv()

        return carry

    lax.fori_loop(0, owners, receive, 0)

    missing = got[0, 4:5, 3 * slots:4 * slots]
    for q in range(1, owners):
        missing = missing + got[q, 4:5, 3 * slots:4 * slots]
    g_order = [gen, gen + 1 - 2 * (gen % 2), 3 - gen, (gen + 2) % 4]
    for pair in range(4):
        halves = []
        for half in range(2):
            q = 2 * pair + half

            def field(sender, n):
                row, lane = LAYERS * (n // 4), slots * (n % 4)
                return got[sender, row:row + LAYERS, lane:lane + slots]

            total = field(q, 0) + field(q ^ 2, 1) + field(q ^ 4, 2) + field(q ^ 6, 3)
            total = total + field(q, 4) + field(q ^ 1, 5)
            flags = field(q, 6)
            density = (total - missing) * math.exp(-8.0)
            halves.append(flags / (density + 1.0 - flags))
        both = jnp.concatenate(halves, axis=1)
        for d in range(LAYERS):
            out[pl.ds(LAYERS * pair + g_order[d], 1), :] = both[d:d + 1, :]

    def sent(j, carry):
        @pl.when(z * owners + j != gen * owners + join)
        def _():
            w_copy(j).wait_send()

        return carry

    lax.fori_loop(0, owners, sent, 0)
    for slot in range(3):
        c_copy(slot).wait_send()
        pltpu.make_async_remote_copy(
            src_ref=snd.at[slot], dst_ref=snd.at[slot], send_sem=zsend.at[slot],
            recv_sem=zrecv.at[0], device_id=y_near, device_id_type=MESH,
        ).wait_send()
    for d in range(LAYERS):
        for kind in (SIB, XN, XS, YN):
            pltpu.make_async_remote_copy(
                src_ref=held.at[d, :, kind], dst_ref=held.at[d, :, kind],
                send_sem=lsend.at[(kind - 1) * LAYERS + d],
                recv_sem=lrecv.at[0], device_id=y_near, device_id_type=MESH,
            ).wait_send()


def layer_body(src_emb, counts):
    block, width = src_emb.shape
    owners = 8
    slots = block // (LAYERS * owners)
    vmem = pl.BlockSpec(memory_space=pltpu.VMEM)
    weights = pl.pallas_call(
        lambda *refs: layer_kernel(slots, width, *refs),
        out_shape=jax.ShapeDtypeStruct((block // 128, 128), jnp.float32),
        in_specs=[pl.BlockSpec(memory_space=pl.ANY)] * 2,
        out_specs=vmem,
        scratch_shapes=[
            pltpu.VMEM((LAYERS, owners * slots, width), jnp.bfloat16),
            pltpu.SMEM((1, 32), jnp.int32),
            pltpu.VMEM((1, 32), jnp.int32),
            pltpu.VMEM((LAYERS, owners, 5, slots, width), jnp.bfloat16),
            pltpu.VMEM((LAYERS - 1, owners, slots, width), jnp.bfloat16),
            pltpu.VMEM((2, LAYERS, 8, owners * slots), jnp.float32),
            pltpu.VMEM((2, LAYERS, owners, 8, 128), jnp.float32),
            pltpu.VMEM((2, 4 * slots, 128), jnp.float32),
            pltpu.VMEM((2, 8, 14 * slots), jnp.float32),
            pltpu.VMEM((owners, 8, 4 * slots), jnp.float32),
            pltpu.VMEM((owners, 8, 4 * slots), jnp.float32),
            pltpu.VMEM((LAYERS, 8, 128), jnp.int32),
            pltpu.SemaphoreType.DMA((LAYERS + 2,)),
            pltpu.SemaphoreType.DMA((3,)),
            pltpu.SemaphoreType.DMA((LAYERS * owners,)),
            pltpu.SemaphoreType.DMA((4 * LAYERS,)),
            pltpu.SemaphoreType.DMA((4 * LAYERS * owners,)),
            pltpu.SemaphoreType.DMA((3,)),
            pltpu.SemaphoreType.DMA((LAYERS,)),
            pltpu.SemaphoreType.DMA((owners,)),
            pltpu.SemaphoreType.DMA((owners,)),
        ],
        compiler_params=pltpu.CompilerParams(
            collective_id=0, has_side_effects=True, vmem_limit_bytes=56 * 2**20
        ),
        name="layer_kernel",
    )(src_emb, counts)
    return weights.reshape(block)


def solution(mesh):
    in_specs = (P(("gen", "join"), None), P(("gen", "join"), None))
    out_specs = P(("gen", "join"))
    fits = mesh.shape["gen"] == 4 and mesh.shape["join"] == 8
    body = layer_body if fits else ring_body
    return jax.shard_map(body, mesh=mesh, in_specs=in_specs, out_specs=out_specs, check_vma=False)
```

```python
import math

import jax
import jax.numpy as jnp
from jax import lax
from jax.experimental import pallas as pl
from jax.experimental.pallas import tpu as pltpu
from jax.sharding import PartitionSpec as P

ROUNDS = 3
MESH = pl.DeviceIdType.MESH
SCALE = 8.0 * math.log2(math.e)
LAYERS = 4
OWN, XN, SIB, XS, YN = range(5)


def shifted(block, axis, distance):
    devices = range(lax.axis_size(axis))
    route = [((i - distance) % len(devices), i) for i in devices]
    return lax.ppermute(block, axis, route)


def tile_sums(left_rows, left_live, right_rows, right_live):
    row_count = left_rows.shape[0]
    piece_rows = min(512, row_count)
    pieces = row_count // piece_rows

    def one_piece(col_total, operands):
        piece_block, piece_live = operands
        scores = lax.dot_general(
            piece_block, right_rows, (((1,), (1,)), ((), ())), preferred_element_type=jnp.float32
        )
        kernel = jnp.exp(8.0 * (scores - 1.0))
        return (
            col_total + jnp.sum(kernel * piece_live[:, None], axis=0),
            jnp.sum(kernel * right_live[None, :], axis=1),
        )

    start_total = jnp.zeros((right_rows.shape[0],), jnp.float32)
    col_sums, row_sums = lax.scan(
        one_piece,
        start_total,
        (
            left_rows.reshape(pieces, piece_rows, left_rows.shape[1]),
            left_live.reshape(pieces, piece_rows),
        ),
    )
    return (row_sums.reshape(row_count), col_sums)


def ring_body(src_emb, counts):
    values = src_emb.astype(jnp.float32)
    width = values.shape[1]
    unit = (
        values
        * lax.rsqrt(jnp.mean(values * values, axis=1, keepdims=True) + 1e-06)
        / math.sqrt(width)
    ).astype(jnp.bfloat16)
    nodes = lax.axis_size(("gen", "join"))
    block_rows = unit.shape[0]
    slots = block_rows // nodes
    received, got_counts = (
        lax.all_to_all(
            unit.reshape(nodes, slots, width),
            ("gen", "join"),
            split_axis=0,
            concat_axis=0,
            tiled=True,
        ),
        lax.all_to_all(
            counts.reshape(nodes), ("gen", "join"), split_axis=0, concat_axis=0, tiled=True
        ),
    )
    owned = received.reshape(block_rows, width)
    slot_index = lax.broadcasted_iota(jnp.int32, (nodes, slots), 1)
    live = (slot_index < got_counts.reshape(nodes, 1)).astype(jnp.float32).reshape(block_rows)
    live_wire = live.astype(jnp.bfloat16)
    density = tile_sums(owned, live, owned, live)[0]
    for shift_by in range(1, ROUNDS + 1):
        other_rows, other_flags = shifted((owned, live_wire), "join", shift_by)
        row_sums, col_sums = tile_sums(owned, live, other_rows, other_flags.astype(jnp.float32))
        density = density + row_sums + shifted(col_sums, "join", -shift_by)
    return live / (density + 1.0 - live)


def layer_kernel(slots, width, src_hbm, counts_hbm, out, src, counts, counts_row, held, snd, racc,
                 dacc, cacc, last, msg, got, live, insem, zsend, zrecv, lsend, lrecv, csend, crecv,
                 wsend, wrecv):
    gen, join = lax.axis_index("gen"), lax.axis_index("join")
    x, k, z, y = gen // 2, gen % 2, join // 2, join % 2
    inner = (z + 1) // 2 % 2
    flip = z + 1 - 2 * (z % 2)
    over = (z + 2) % 4
    far = 3 - z
    owners = 8
    rows = owners * slots
    tall = 4 * slots
    pieces = LAYERS * owners
    peers = [flip, far, over]
    sibling = (2 * x + 1 - k, join)
    x_near = (2 * (1 - x) + k, join)
    y_near = (gen, 2 * z + 1 - y)

    barrier = pltpu.get_barrier_semaphore()
    for peer in (
        (gen, 2 * flip + y), (gen, 2 * over + y), (gen, 2 * far + y), x_near, y_near, sibling
    ):
        pl.semaphore_signal(barrier, inc=1, device_id=peer, device_id_type=MESH)

    loads = [
        pltpu.make_async_copy(counts_hbm, counts, insem.at[LAYERS]),
        pltpu.make_async_copy(counts_hbm, counts_row, insem.at[LAYERS + 1]),
    ]
    for n, layer in enumerate([z] + peers):
        start = pl.multiple_of(layer * rows, rows)
        loads.append(
            pltpu.make_async_copy(src_hbm.at[pl.ds(start, rows)], src.at[n], insem.at[n])
        )
    for load in loads:
        load.start()

    def normalize(n, layer, b, into):
        start = pl.multiple_of(b * slots, slots)
        values = src[n, pl.ds(start, slots), :].astype(jnp.float32)
        spare = (counts[0, layer * owners + b]
                 - lax.broadcasted_iota(jnp.int32, (slots, 1), 0)).astype(jnp.float32)
        alive = jnp.clip(spare, 0.0, 1.0)
        factor = lax.rsqrt(jnp.mean(values * values, axis=1, keepdims=True) + 1e-06)
        into[...] = (values * (factor * (alive / math.sqrt(width)))).astype(jnp.bfloat16)

    def z_copy(slot, b):
        return pltpu.make_async_remote_copy(
            src_ref=snd.at[slot, b], dst_ref=held.at[slot + 1, b, OWN],
            send_sem=zsend.at[slot], recv_sem=zrecv.at[(slot + 1) * owners + b],
            device_id=(gen, 2 * peers[slot] + y), device_id_type=MESH,
        )

    def c_copy(slot):
        return pltpu.make_async_remote_copy(
            src_ref=live.at[0], dst_ref=live.at[slot + 1], send_sem=csend.at[slot],
            recv_sem=crecv.at[slot + 1], device_id=(gen, 2 * peers[slot] + y),
            device_id_type=MESH,
        )

    def l_copy(t, kind):
        d, b = t // owners, t % owners
        target = {XN: x_near, YN: y_near}[kind]
        way = kind // YN
        return pltpu.make_async_remote_copy(
            src_ref=held.at[d, b, OWN], dst_ref=held.at[d, b, kind],
            send_sem=lsend.at[way * LAYERS + d], recv_sem=lrecv.at[way * pieces + t],
            device_id=target, device_id_type=MESH,
        )

    def s_copy(t):
        d, b = t // owners, t % owners
        return pltpu.make_async_remote_copy(
            src_ref=held.at[d, b, pl.ds(OWN, 2)], dst_ref=held.at[d, b, pl.ds(SIB, 2)],
            send_sem=lsend.at[2 * LAYERS + d], recv_sem=lrecv.at[2 * pieces + t],
            device_id=sibling, device_id_type=MESH,
        )

    def spread(t):
        l_copy(t, XN).start()
        l_copy(t, YN).start()

    def arrive(t):
        d, b = t // owners, t % owners
        pltpu.make_async_remote_copy(
            src_ref=snd.at[0, 0], dst_ref=held.at[d, b, OWN],
            send_sem=zsend.at[0], recv_sem=zrecv.at[t],
            device_id=y_near, device_id_type=MESH,
        ).wait_recv()
        spread(t)

    def relay(t):
        l_copy(t, XN).wait_recv()
        s_copy(t).start()

    def normalize_slot(slot):
        def one(b, carry):
            normalize(slot + 1, peers[slot], b, snd.at[slot, b])
            return carry

        loads[slot + 3].wait()
        lax.fori_loop(0, owners, one, 0)

    def own_piece(b, carry):
        normalize(0, z, b, held.at[0, b, OWN])
        return carry

    for load in loads[:3]:
        load.wait()
    lax.fori_loop(0, owners, own_piece, 0)
    normalize_slot(0)
    normalize_slot(1)
    live[0] = jnp.zeros((8, 128), jnp.int32)
    live[0, 0:1, 0:32] = counts_row[...]
    pl.semaphore_wait(barrier, 6)

    for slot in range(3):
        c_copy(slot).start()

    def first(b, carry):
        @pl.when(inner == 1)
        def _():
            z_copy(1, b).start()

        z_copy(0, b).start()
        spread(b)
        return carry

    lax.fori_loop(0, owners, first, 0)
    normalize_slot(2)

    def second(b, carry):
        @pl.when(inner == 0)
        def _():
            z_copy(1, b).start()

        z_copy(2, b).start()
        return carry

    lax.fori_loop(0, owners, second, 0)
    racc[...] = jnp.zeros_like(racc)
    dacc[...] = jnp.zeros_like(dacc)
    cacc[...] = jnp.zeros_like(cacc)
    last[...] = jnp.zeros_like(last)

    lane_owner = lax.broadcasted_iota(jnp.int32, (1, rows), 1) // slots
    ones = jnp.ones((16, 128), jnp.bfloat16)

    turns = [(r, m) for r in range(2) for m in (0, 1, 2, 3, 5, 6, 7)]
    turn = lax.broadcasted_iota(jnp.int32, (1, len(turns) * slots), 1) // slots % 7
    turn = turn + turn // 4
    zero_one = jnp.minimum(turn, 1).astype(jnp.float32)

    def earlier(b, m):
        return (b - m) * ((b - m + owners) // owners)

    def settle(t):
        d, b = t // owners, t % owners
        sums = cacc[t % 2]
        high = sums.astype(jnp.bfloat16)
        low = (sums - high.astype(jnp.float32)).astype(jnp.bfloat16)
        flat = (((1,), (1,)), ((), ()))
        line = lax.dot_general(ones, high, flat, preferred_element_type=jnp.float32)
        line += lax.dot_general(ones, low, flat, preferred_element_type=jnp.float32)
        msg[b, pl.ds(d, 1), :] = line[0:1, :]
        for n, (r, m) in enumerate(turns):
            dacc[r, d, earlier(b, m), :, 0:slots] += last[t % 2, :, n * slots:(n + 1) * slots]

    def kernel_of(left, right):
        scores = lax.dot_general(
            left, right, (((1,), (1,)), ((), ())), preferred_element_type=jnp.float32
        )
        return jnp.exp2(scores * SCALE)

    def down(values):
        return jnp.sum(values.reshape(values.shape[0] // 8, 8, values.shape[1]), axis=0)

    def across(values):
        total = values[:, 0:128]
        for c in range(1, values.shape[1] // 128):
            total = total + values[:, 128 * c:128 * (c + 1)]
        return total

    def tile(d, b):
        left = held[d, b, 0:4].reshape(tall, width)
        right = jnp.concatenate(
            [held[d, earlier(b, m), (OWN, YN)[r]] for r, m in turns], axis=0
        )
        kernel = kernel_of(left, right)
        use = jnp.where(turn <= b, 1.0, 0.0)
        last[(d * owners + b) % 2] = down(kernel) * use
        total = across(kernel * (use * zero_one))
        near = jnp.where(lane_owner != (b + 4) % owners, 1.0, 0.0)
        for i in range(d):
            for r, kind in enumerate((OWN, YN)):
                kernel = kernel_of(left, held[i, :, kind].reshape(rows, width))
                racc[r, i] += down(kernel) * near
                total = total + across(kernel * near)
        cacc[(d * owners + b) % 2] = total

    def follow(d, b, ahead, next_up):
        t = d * owners + b
        if ahead:
            arrive(t + 4)
        if next_up:
            relay(t + 1)
        l_copy(t, YN).wait_recv()
        s_copy(t).wait_recv()
        settle((t + pieces - 1) % pieces)
        tile(d, b)

    relay(0)
    for d in range(LAYERS):
        spans = {0: (0, 4, 8), 1: (0, 8), 2: (0, 8), 3: (0, 4, 7, 8)}[d]
        for start, stop in zip(spans, spans[1:]):
            ahead = start >= 4 if d == 0 else d < 3 or start == 0

            def step(b, carry):
                follow(d, b, ahead, stop < owners or d < 3)
                return carry

            lax.fori_loop(start, stop, step, 0)
        if d == 1:
            for place in range(1, LAYERS):
                pltpu.make_async_remote_copy(
                    src_ref=live.at[0], dst_ref=live.at[place], send_sem=csend.at[0],
                    recv_sem=crecv.at[place], device_id=y_near, device_id_type=MESH,
                ).wait_recv()
            lane = lax.broadcasted_iota(jnp.int32, (owners, 128), 1)
            mine = owners * z + lax.broadcasted_iota(jnp.int32, (owners, 128), 0)
            across_of = owners * z + (4 + lax.broadcasted_iota(jnp.int32, (owners, 128), 0)) % owners
            group = (lane >= owners * z) & (lane < owners * z + owners) & (lane != across_of)
            slot_index = lax.broadcasted_iota(jnp.int32, (owners, slots), 1).astype(jnp.float32)
            dead = jnp.zeros((owners, 128), jnp.float32)
            for place in range(LAYERS):
                filled = jnp.broadcast_to(live[place, 0:1, :].astype(jnp.float32), (owners, 128))
                limit = jnp.sum(jnp.where(lane == mine, filled, 0.0), axis=1, keepdims=True)
                flags = jnp.where(slot_index < limit, 1.0, 0.0)
                for j in range(owners):
                    msg[j, 4 + place:5 + place, 2 * slots:3 * slots] = flags[j:j + 1, :]
                dead = dead + jnp.where(group, float(slots) - filled, 0.0)
            missing = jnp.broadcast_to(jnp.sum(dead, axis=1, keepdims=True), (owners, slots))
            for j in range(owners):
                msg[j, 4:5, 3 * slots:4 * slots] = missing[j:j + 1, :]

    settle(pieces - 1)
    for r in range(2):
        for d in range(LAYERS):
            line = jnp.sum(racc[r, d], axis=0, keepdims=True)
            for j in range(owners):
                extra = jnp.sum(dacc[r, d, j, :, 0:slots], axis=0, keepdims=True)
                msg[j, 4 + d:5 + d, r * slots:(1 + r) * slots] = (
                    line[:, j * slots:(j + 1) * slots] + extra
                )

    spot = 2 * gen + y

    def w_copy(j):
        return pltpu.make_async_remote_copy(
            src_ref=msg.at[j], dst_ref=got.at[spot], send_sem=wsend.at[j],
            recv_sem=wrecv.at[spot], device_id=(z, j), device_id_type=MESH,
        )

    def send(j, carry):
        @pl.when(z * owners + j != gen * owners + join)
        def _():
            w_copy(j).start()

        @pl.when(z * owners + j == gen * owners + join)
        def _():
            got[spot] = msg[j]

        return carry

    lax.fori_loop(0, owners, send, 0)

    def receive(i, carry):
        @pl.when((i // 2) * owners + 2 * gen + i % 2 != gen * owners + join)
        def _():
            pltpu.make_async_remote_copy(
                src_ref=msg.at[0], dst_ref=got.at[i], send_sem=wsend.at[0],
                recv_sem=wrecv.at[i], device_id=y_near, device_id_type=MESH,
            ).wait_recv()

        return carry

    lax.fori_loop(0, owners, receive, 0)

    missing = got[0, 4:5, 3 * slots:4 * slots]
    for q in range(1, owners):
        missing = missing + got[q, 4:5, 3 * slots:4 * slots]
    g_order = [gen, gen + 1 - 2 * (gen % 2), 3 - gen, (gen + 2) % 4]
    for pair in range(4):
        halves = []
        for half in range(2):
            q = 2 * pair + half

            def field(sender, n):
                row, lane = LAYERS * (n // 4), slots * (n % 4)
                return got[sender, row:row + LAYERS, lane:lane + slots]

            total = field(q, OWN) + field(q ^ 4, XN) + field(q ^ 2, SIB) + field(q ^ 6, XS)
            total = total + field(q, 4) + field(q ^ 1, 5)
            flags = field(q, 6)
            density = (total - missing) * math.exp(-8.0)
            halves.append(flags / (density + 1.0 - flags))
        both = jnp.concatenate(halves, axis=1)
        for d in range(LAYERS):
            out[pl.ds(LAYERS * pair + g_order[d], 1), :] = both[d:d + 1, :]

    def sent(j, carry):
        @pl.when(z * owners + j != gen * owners + join)
        def _():
            w_copy(j).wait_send()

        return carry

    lax.fori_loop(0, owners, sent, 0)
    for slot in range(3):
        c_copy(slot).wait_send()
        pltpu.make_async_remote_copy(
            src_ref=snd.at[slot], dst_ref=snd.at[slot], send_sem=zsend.at[slot],
            recv_sem=zrecv.at[0], device_id=y_near, device_id_type=MESH,
        ).wait_send()
    for d in range(LAYERS):
        for way in range(3):
            place = (pl.ds(OWN, 1), pl.ds(OWN, 1), pl.ds(OWN, 2))[way]
            pltpu.make_async_remote_copy(
                src_ref=held.at[d, :, place], dst_ref=held.at[d, :, place],
                send_sem=lsend.at[way * LAYERS + d], recv_sem=lrecv.at[0],
                device_id=y_near, device_id_type=MESH,
            ).wait_send()


def layer_body(src_emb, counts):
    block, width = src_emb.shape
    owners = 8
    slots = block // (LAYERS * owners)
    vmem = pl.BlockSpec(memory_space=pltpu.VMEM)
    weights = pl.pallas_call(
        lambda *refs: layer_kernel(slots, width, *refs),
        out_shape=jax.ShapeDtypeStruct((block // 128, 128), jnp.float32),
        in_specs=[pl.BlockSpec(memory_space=pl.ANY)] * 2,
        out_specs=vmem,
        scratch_shapes=[
            pltpu.VMEM((LAYERS, owners * slots, width), jnp.bfloat16),
            pltpu.SMEM((1, 32), jnp.int32),
            pltpu.VMEM((1, 32), jnp.int32),
            pltpu.VMEM((LAYERS, owners, 5, slots, width), jnp.bfloat16),
            pltpu.VMEM((LAYERS - 1, owners, slots, width), jnp.bfloat16),
            pltpu.VMEM((2, LAYERS, 8, owners * slots), jnp.float32),
            pltpu.VMEM((2, LAYERS, owners, 8, 128), jnp.float32),
            pltpu.VMEM((2, 4 * slots, 128), jnp.float32),
            pltpu.VMEM((2, 8, 14 * slots), jnp.float32),
            pltpu.VMEM((owners, 8, 4 * slots), jnp.float32),
            pltpu.VMEM((owners, 8, 4 * slots), jnp.float32),
            pltpu.VMEM((LAYERS, 8, 128), jnp.int32),
            pltpu.SemaphoreType.DMA((LAYERS + 2,)),
            pltpu.SemaphoreType.DMA((3,)),
            pltpu.SemaphoreType.DMA((LAYERS * owners,)),
            pltpu.SemaphoreType.DMA((3 * LAYERS,)),
            pltpu.SemaphoreType.DMA((3 * LAYERS * owners,)),
            pltpu.SemaphoreType.DMA((3,)),
            pltpu.SemaphoreType.DMA((LAYERS,)),
            pltpu.SemaphoreType.DMA((owners,)),
            pltpu.SemaphoreType.DMA((owners,)),
        ],
        compiler_params=pltpu.CompilerParams(
            collective_id=0, has_side_effects=True, vmem_limit_bytes=56 * 2**20
        ),
        name="layer_kernel",
    )(src_emb, counts)
    return weights.reshape(block)


def solution(mesh):
    in_specs = (P(("gen", "join"), None), P(("gen", "join"), None))
    out_specs = P(("gen", "join"))
    fits = mesh.shape["gen"] == 4 and mesh.shape["join"] == 8
    body = layer_body if fits else ring_body
    return jax.shard_map(body, mesh=mesh, in_specs=in_specs, out_specs=out_specs, check_vma=False)
```

```python
import math

import jax
import jax.numpy as jnp
from jax import lax
from jax.experimental import pallas as pl
from jax.experimental.pallas import tpu as pltpu
from jax.sharding import PartitionSpec as P

ROUNDS = 3
MESH = pl.DeviceIdType.MESH
SCALE = 8.0 * math.log2(math.e)
LAYERS = 4
OWN, XN, SIB, XS, YN = range(5)


def shifted(block, axis, distance):
    devices = range(lax.axis_size(axis))
    route = [((i - distance) % len(devices), i) for i in devices]
    return lax.ppermute(block, axis, route)


def tile_sums(left_rows, left_live, right_rows, right_live):
    row_count = left_rows.shape[0]
    piece_rows = min(512, row_count)
    pieces = row_count // piece_rows

    def one_piece(col_total, operands):
        piece_block, piece_live = operands
        scores = lax.dot_general(
            piece_block, right_rows, (((1,), (1,)), ((), ())), preferred_element_type=jnp.float32
        )
        kernel = jnp.exp(8.0 * (scores - 1.0))
        return (
            col_total + jnp.sum(kernel * piece_live[:, None], axis=0),
            jnp.sum(kernel * right_live[None, :], axis=1),
        )

    start_total = jnp.zeros((right_rows.shape[0],), jnp.float32)
    col_sums, row_sums = lax.scan(
        one_piece,
        start_total,
        (
            left_rows.reshape(pieces, piece_rows, left_rows.shape[1]),
            left_live.reshape(pieces, piece_rows),
        ),
    )
    return (row_sums.reshape(row_count), col_sums)


def ring_body(src_emb, counts):
    values = src_emb.astype(jnp.float32)
    width = values.shape[1]
    unit = (
        values
        * lax.rsqrt(jnp.mean(values * values, axis=1, keepdims=True) + 1e-06)
        / math.sqrt(width)
    ).astype(jnp.bfloat16)
    nodes = lax.axis_size(("gen", "join"))
    block_rows = unit.shape[0]
    slots = block_rows // nodes
    received, got_counts = (
        lax.all_to_all(
            unit.reshape(nodes, slots, width),
            ("gen", "join"),
            split_axis=0,
            concat_axis=0,
            tiled=True,
        ),
        lax.all_to_all(
            counts.reshape(nodes), ("gen", "join"), split_axis=0, concat_axis=0, tiled=True
        ),
    )
    owned = received.reshape(block_rows, width)
    slot_index = lax.broadcasted_iota(jnp.int32, (nodes, slots), 1)
    live = (slot_index < got_counts.reshape(nodes, 1)).astype(jnp.float32).reshape(block_rows)
    live_wire = live.astype(jnp.bfloat16)
    density = tile_sums(owned, live, owned, live)[0]
    for shift_by in range(1, ROUNDS + 1):
        other_rows, other_flags = shifted((owned, live_wire), "join", shift_by)
        row_sums, col_sums = tile_sums(owned, live, other_rows, other_flags.astype(jnp.float32))
        density = density + row_sums + shifted(col_sums, "join", -shift_by)
    return live / (density + 1.0 - live)


def layer_kernel(slots, width, src_hbm, counts_hbm, out, src, counts, counts_row, held, snd, racc,
                 dacc, cacc, last, msg, got, live, insem, zsend, zrecv, lsend, lrecv, csend, crecv,
                 wsend, wrecv):
    gen, join = lax.axis_index("gen"), lax.axis_index("join")
    x, k, z, y = gen // 2, gen % 2, join // 2, join % 2
    inner = (z + 1) // 2 % 2
    flip = z + 1 - 2 * (z % 2)
    over = (z + 2) % 4
    far = 3 - z
    owners = 8
    rows = owners * slots
    tall = 4 * slots
    pieces = LAYERS * owners
    peers = [flip, far, over]
    sibling = (2 * x + 1 - k, join)
    x_near = (2 * (1 - x) + k, join)
    y_near = (gen, 2 * z + 1 - y)

    barrier = pltpu.get_barrier_semaphore()
    for peer in (
        (gen, 2 * flip + y), (gen, 2 * over + y), (gen, 2 * far + y), x_near, y_near, sibling
    ):
        pl.semaphore_signal(barrier, inc=1, device_id=peer, device_id_type=MESH)

    loads = [
        pltpu.make_async_copy(counts_hbm, counts, insem.at[LAYERS]),
        pltpu.make_async_copy(counts_hbm, counts_row, insem.at[LAYERS + 1]),
    ]
    for n, layer in enumerate([z] + peers):
        start = pl.multiple_of(layer * rows, rows)
        loads.append(
            pltpu.make_async_copy(src_hbm.at[pl.ds(start, rows)], src.at[n], insem.at[n])
        )
    for load in loads:
        load.start()

    def normalize(n, layer, b, into):
        start = pl.multiple_of(b * slots, slots)
        values = src[n, pl.ds(start, slots), :].astype(jnp.float32)
        spare = (counts[0, layer * owners + b]
                 - lax.broadcasted_iota(jnp.int32, (slots, 1), 0)).astype(jnp.float32)
        alive = jnp.clip(spare, 0.0, 1.0)
        factor = lax.rsqrt(jnp.mean(values * values, axis=1, keepdims=True) + 1e-06)
        into[...] = (values * (factor * (alive / math.sqrt(width)))).astype(jnp.bfloat16)

    def z_copy(slot, b):
        return pltpu.make_async_remote_copy(
            src_ref=snd.at[slot, b], dst_ref=held.at[slot + 1, b, OWN],
            send_sem=zsend.at[slot], recv_sem=zrecv.at[(slot + 1) * owners + b],
            device_id=(gen, 2 * peers[slot] + y), device_id_type=MESH,
        )

    def c_copy(slot):
        return pltpu.make_async_remote_copy(
            src_ref=live.at[0], dst_ref=live.at[slot + 1], send_sem=csend.at[slot],
            recv_sem=crecv.at[slot + 1], device_id=(gen, 2 * peers[slot] + y),
            device_id_type=MESH,
        )

    def l_copy(t, kind):
        d, b = t // owners, t % owners
        target = {XN: x_near, YN: y_near}[kind]
        way = kind // YN
        return pltpu.make_async_remote_copy(
            src_ref=held.at[d, b, OWN], dst_ref=held.at[d, b, kind],
            send_sem=lsend.at[way * LAYERS + d], recv_sem=lrecv.at[way * pieces + t],
            device_id=target, device_id_type=MESH,
        )

    def s_copy(t):
        d, b = t // owners, t % owners
        return pltpu.make_async_remote_copy(
            src_ref=held.at[d, b, pl.ds(OWN, 2)], dst_ref=held.at[d, b, pl.ds(SIB, 2)],
            send_sem=lsend.at[2 * LAYERS + d], recv_sem=lrecv.at[2 * pieces + t],
            device_id=sibling, device_id_type=MESH,
        )

    def spread(t):
        l_copy(t, XN).start()
        l_copy(t, YN).start()

    def arrive(t):
        d, b = t // owners, t % owners
        pltpu.make_async_remote_copy(
            src_ref=snd.at[0, 0], dst_ref=held.at[d, b, OWN],
            send_sem=zsend.at[0], recv_sem=zrecv.at[t],
            device_id=y_near, device_id_type=MESH,
        ).wait_recv()
        spread(t)

    def relay(t):
        l_copy(t, XN).wait_recv()
        s_copy(t).start()

    def normalize_slot(slot):
        def one(b, carry):
            normalize(slot + 1, peers[slot], b, snd.at[slot, b])
            return carry

        loads[slot + 3].wait()
        lax.fori_loop(0, owners, one, 0)

    def own_piece(b, carry):
        normalize(0, z, b, held.at[0, b, OWN])
        return carry

    for load in loads[:3]:
        load.wait()
    lax.fori_loop(0, owners, own_piece, 0)
    normalize_slot(0)
    normalize_slot(1)
    live[0] = jnp.zeros((8, 128), jnp.int32)
    live[0, 0:1, 0:32] = counts_row[...]
    pl.semaphore_wait(barrier, 6)

    for slot in range(3):
        c_copy(slot).start()

    def first(b, carry):
        @pl.when(inner == 1)
        def _():
            z_copy(1, b).start()

        z_copy(0, b).start()
        spread(b)
        return carry

    lax.fori_loop(0, owners, first, 0)
    normalize_slot(2)

    def second(b, carry):
        @pl.when(inner == 0)
        def _():
            z_copy(1, b).start()

        z_copy(2, b).start()
        return carry

    lax.fori_loop(0, owners, second, 0)
    racc[...] = jnp.zeros_like(racc)
    dacc[...] = jnp.zeros_like(dacc)
    cacc[...] = jnp.zeros_like(cacc)
    last[...] = jnp.zeros_like(last)

    lane_owner = lax.broadcasted_iota(jnp.int32, (1, rows), 1) // slots
    ones = jnp.ones((256, 128), jnp.bfloat16)
    diagonal = (
        lax.broadcasted_iota(jnp.int32, (128, 128), 0)
        == lax.broadcasted_iota(jnp.int32, (128, 128), 1)
    )

    turns = [(r, m) for r in range(2) for m in (0, 1, 2, 3, 5, 6, 7)]
    turn = lax.broadcasted_iota(jnp.int32, (1, len(turns) * slots), 1) // slots % 7
    turn = turn + turn // 4
    zero_one = jnp.minimum(turn, 1).astype(jnp.float32)

    def earlier(b, m):
        return (b - m) * ((b - m + owners) // owners)

    def settle(t):
        d, b = t // owners, t % owners
        sums = cacc[t % 2]
        high = sums.astype(jnp.bfloat16)
        low = (sums - high.astype(jnp.float32)).astype(jnp.bfloat16)
        summed = lax.dot_general(
            jnp.concatenate([high, low], axis=1), ones, (((1,), (0,)), ((), ())),
            preferred_element_type=jnp.float32,
        )
        line = jnp.concatenate([
            jnp.sum(jnp.where(diagonal, summed[c:c + 128, :], 0.0), axis=0, keepdims=True)
            for c in range(0, tall, 128)
        ], axis=1)
        msg[b, pl.ds(d, 1), :] = line
        for n, (r, m) in enumerate(turns):
            dacc[r, d, earlier(b, m), :, 0:slots] += last[t % 2, :, n * slots:(n + 1) * slots]

    def kernel_of(left, right):
        scores = lax.dot_general(
            left, right, (((1,), (1,)), ((), ())), preferred_element_type=jnp.float32
        )
        return jnp.exp2(scores * SCALE)

    def down(values):
        return jnp.sum(values.reshape(values.shape[0] // 8, 8, values.shape[1]), axis=0)

    def across(values):
        total = values[:, 0:128]
        for c in range(1, values.shape[1] // 128):
            total = total + values[:, 128 * c:128 * (c + 1)]
        return total

    def tile(d, b):
        left = held[d, b, 0:4].reshape(tall, width)
        total = jnp.zeros((tall, 128), jnp.float32)
        near = jnp.where(lane_owner != (b + 4) % owners, 1.0, 0.0)
        for i in range(d):
            for r, kind in enumerate((OWN, YN)):
                kernel = kernel_of(left, held[i, :, kind].reshape(rows, width))
                racc[r, i] += down(kernel) * near
                total = total + across(kernel * near)
        right = jnp.concatenate(
            [held[d, earlier(b, m), (OWN, YN)[r]] for r, m in turns], axis=0
        )
        kernel = kernel_of(left, right)
        use = jnp.where(turn <= b, 1.0, 0.0)
        last[(d * owners + b) % 2] = down(kernel) * use
        total = total + across(kernel * (use * zero_one))
        cacc[(d * owners + b) % 2] = total

    def follow(d, b, ahead, next_up):
        t = d * owners + b
        if ahead:
            arrive(t + 4)
        if next_up:
            relay(t + 1)
        l_copy(t, YN).wait_recv()
        s_copy(t).wait_recv()
        settle((t + pieces - 1) % pieces)
        tile(d, b)

    relay(0)
    for d in range(LAYERS):
        spans = {0: (0, 4, 8), 1: (0, 8), 2: (0, 8), 3: (0, 4, 7, 8)}[d]
        for start, stop in zip(spans, spans[1:]):
            ahead = start >= 4 if d == 0 else d < 3 or start == 0

            def step(b, carry):
                follow(d, b, ahead, stop < owners or d < 3)
                return carry

            lax.fori_loop(start, stop, step, 0)
        if d == 1:
            for place in range(1, LAYERS):
                pltpu.make_async_remote_copy(
                    src_ref=live.at[0], dst_ref=live.at[place], send_sem=csend.at[0],
                    recv_sem=crecv.at[place], device_id=y_near, device_id_type=MESH,
                ).wait_recv()
            lane = lax.broadcasted_iota(jnp.int32, (owners, 128), 1)
            mine = owners * z + lax.broadcasted_iota(jnp.int32, (owners, 128), 0)
            across_of = owners * z + (4 + lax.broadcasted_iota(jnp.int32, (owners, 128), 0)) % owners
            group = (lane >= owners * z) & (lane < owners * z + owners) & (lane != across_of)
            slot_index = lax.broadcasted_iota(jnp.int32, (owners, slots), 1).astype(jnp.float32)
            dead = jnp.zeros((owners, 128), jnp.float32)
            for place in range(LAYERS):
                filled = jnp.broadcast_to(live[place, 0:1, :].astype(jnp.float32), (owners, 128))
                limit = jnp.sum(jnp.where(lane == mine, filled, 0.0), axis=1, keepdims=True)
                flags = jnp.where(slot_index < limit, 1.0, 0.0)
                for j in range(owners):
                    msg[j, 4 + place:5 + place, 2 * slots:3 * slots] = flags[j:j + 1, :]
                dead = dead + jnp.where(group, float(slots) - filled, 0.0)
            missing = jnp.broadcast_to(jnp.sum(dead, axis=1, keepdims=True), (owners, slots))
            for j in range(owners):
                msg[j, 4:5, 3 * slots:4 * slots] = missing[j:j + 1, :]

    settle(pieces - 1)
    for r in range(2):
        for d in range(LAYERS):
            line = jnp.sum(racc[r, d], axis=0, keepdims=True)
            for j in range(owners):
                extra = jnp.sum(dacc[r, d, j, :, 0:slots], axis=0, keepdims=True)
                msg[j, 4 + d:5 + d, r * slots:(1 + r) * slots] = (
                    line[:, j * slots:(j + 1) * slots] + extra
                )

    spot = 2 * gen + y

    def w_copy(j):
        return pltpu.make_async_remote_copy(
            src_ref=msg.at[j], dst_ref=got.at[spot], send_sem=wsend.at[j],
            recv_sem=wrecv.at[spot], device_id=(z, j), device_id_type=MESH,
        )

    def send(j, carry):
        @pl.when(z * owners + j != gen * owners + join)
        def _():
            w_copy(j).start()

        @pl.when(z * owners + j == gen * owners + join)
        def _():
            got[spot] = msg[j]

        return carry

    lax.fori_loop(0, owners, send, 0)

    def receive(i, carry):
        @pl.when((i // 2) * owners + 2 * gen + i % 2 != gen * owners + join)
        def _():
            pltpu.make_async_remote_copy(
                src_ref=msg.at[0], dst_ref=got.at[i], send_sem=wsend.at[0],
                recv_sem=wrecv.at[i], device_id=y_near, device_id_type=MESH,
            ).wait_recv()

        return carry

    lax.fori_loop(0, owners, receive, 0)

    missing = got[0, 4:5, 3 * slots:4 * slots]
    for q in range(1, owners):
        missing = missing + got[q, 4:5, 3 * slots:4 * slots]
    g_order = [gen, gen + 1 - 2 * (gen % 2), 3 - gen, (gen + 2) % 4]
    for pair in range(4):
        halves = []
        for half in range(2):
            q = 2 * pair + half

            def field(sender, n):
                row, lane = LAYERS * (n // 4), slots * (n % 4)
                return got[sender, row:row + LAYERS, lane:lane + slots]

            total = field(q, OWN) + field(q ^ 4, XN) + field(q ^ 2, SIB) + field(q ^ 6, XS)
            total = total + field(q, 4) + field(q ^ 1, 5)
            flags = field(q, 6)
            density = (total - missing) * math.exp(-8.0)
            halves.append(flags / (density + 1.0 - flags))
        both = jnp.concatenate(halves, axis=1)
        for d in range(LAYERS):
            out[pl.ds(LAYERS * pair + g_order[d], 1), :] = both[d:d + 1, :]

    def sent(j, carry):
        @pl.when(z * owners + j != gen * owners + join)
        def _():
            w_copy(j).wait_send()

        return carry

    lax.fori_loop(0, owners, sent, 0)
    for slot in range(3):
        c_copy(slot).wait_send()
        pltpu.make_async_remote_copy(
            src_ref=snd.at[slot], dst_ref=snd.at[slot], send_sem=zsend.at[slot],
            recv_sem=zrecv.at[0], device_id=y_near, device_id_type=MESH,
        ).wait_send()
    for d in range(LAYERS):
        for way in range(3):
            place = (pl.ds(OWN, 1), pl.ds(OWN, 1), pl.ds(OWN, 2))[way]
            pltpu.make_async_remote_copy(
                src_ref=held.at[d, :, place], dst_ref=held.at[d, :, place],
                send_sem=lsend.at[way * LAYERS + d], recv_sem=lrecv.at[0],
                device_id=y_near, device_id_type=MESH,
            ).wait_send()


def layer_body(src_emb, counts):
    block, width = src_emb.shape
    owners = 8
    slots = block // (LAYERS * owners)
    vmem = pl.BlockSpec(memory_space=pltpu.VMEM)
    weights = pl.pallas_call(
        lambda *refs: layer_kernel(slots, width, *refs),
        out_shape=jax.ShapeDtypeStruct((block // 128, 128), jnp.float32),
        in_specs=[pl.BlockSpec(memory_space=pl.ANY)] * 2,
        out_specs=vmem,
        scratch_shapes=[
            pltpu.VMEM((LAYERS, owners * slots, width), jnp.bfloat16),
            pltpu.SMEM((1, 32), jnp.int32),
            pltpu.VMEM((1, 32), jnp.int32),
            pltpu.VMEM((LAYERS, owners, 5, slots, width), jnp.bfloat16),
            pltpu.VMEM((LAYERS - 1, owners, slots, width), jnp.bfloat16),
            pltpu.VMEM((2, LAYERS, 8, owners * slots), jnp.float32),
            pltpu.VMEM((2, LAYERS, owners, 8, 128), jnp.float32),
            pltpu.VMEM((2, 4 * slots, 128), jnp.float32),
            pltpu.VMEM((2, 8, 14 * slots), jnp.float32),
            pltpu.VMEM((owners, 8, 4 * slots), jnp.float32),
            pltpu.VMEM((owners, 8, 4 * slots), jnp.float32),
            pltpu.VMEM((LAYERS, 8, 128), jnp.int32),
            pltpu.SemaphoreType.DMA((LAYERS + 2,)),
            pltpu.SemaphoreType.DMA((3,)),
            pltpu.SemaphoreType.DMA((LAYERS * owners,)),
            pltpu.SemaphoreType.DMA((3 * LAYERS,)),
            pltpu.SemaphoreType.DMA((3 * LAYERS * owners,)),
            pltpu.SemaphoreType.DMA((3,)),
            pltpu.SemaphoreType.DMA((LAYERS,)),
            pltpu.SemaphoreType.DMA((owners,)),
            pltpu.SemaphoreType.DMA((owners,)),
        ],
        compiler_params=pltpu.CompilerParams(
            collective_id=0, has_side_effects=True, vmem_limit_bytes=56 * 2**20
        ),
        name="layer_kernel",
    )(src_emb, counts)
    return weights.reshape(block)


def solution(mesh):
    in_specs = (P(("gen", "join"), None), P(("gen", "join"), None))
    out_specs = P(("gen", "join"))
    fits = mesh.shape["gen"] == 4 and mesh.shape["join"] == 8
    body = layer_body if fits else ring_body
    return jax.shard_map(body, mesh=mesh, in_specs=in_specs, out_specs=out_specs, check_vma=False)
```

```python
import math

import jax
import jax.numpy as jnp
from jax import lax
from jax.experimental import pallas as pl
from jax.experimental.pallas import tpu as pltpu
from jax.sharding import PartitionSpec as P

ROUNDS = 3
MESH = pl.DeviceIdType.MESH
SCALE = 8.0 * math.log2(math.e)
LAYERS = 4
OWN, XN, SIB, XS, YN = range(5)


def shifted(block, axis, distance):
    devices = range(lax.axis_size(axis))
    route = [((i - distance) % len(devices), i) for i in devices]
    return lax.ppermute(block, axis, route)


def tile_sums(left_rows, left_live, right_rows, right_live):
    row_count = left_rows.shape[0]
    piece_rows = min(512, row_count)
    pieces = row_count // piece_rows

    def one_piece(col_total, operands):
        piece_block, piece_live = operands
        scores = lax.dot_general(
            piece_block, right_rows, (((1,), (1,)), ((), ())), preferred_element_type=jnp.float32
        )
        kernel = jnp.exp(8.0 * (scores - 1.0))
        return (
            col_total + jnp.sum(kernel * piece_live[:, None], axis=0),
            jnp.sum(kernel * right_live[None, :], axis=1),
        )

    start_total = jnp.zeros((right_rows.shape[0],), jnp.float32)
    col_sums, row_sums = lax.scan(
        one_piece,
        start_total,
        (
            left_rows.reshape(pieces, piece_rows, left_rows.shape[1]),
            left_live.reshape(pieces, piece_rows),
        ),
    )
    return (row_sums.reshape(row_count), col_sums)


def ring_body(src_emb, counts):
    values = src_emb.astype(jnp.float32)
    width = values.shape[1]
    unit = (
        values
        * lax.rsqrt(jnp.mean(values * values, axis=1, keepdims=True) + 1e-06)
        / math.sqrt(width)
    ).astype(jnp.bfloat16)
    nodes = lax.axis_size(("gen", "join"))
    block_rows = unit.shape[0]
    slots = block_rows // nodes
    received, got_counts = (
        lax.all_to_all(
            unit.reshape(nodes, slots, width),
            ("gen", "join"),
            split_axis=0,
            concat_axis=0,
            tiled=True,
        ),
        lax.all_to_all(
            counts.reshape(nodes), ("gen", "join"), split_axis=0, concat_axis=0, tiled=True
        ),
    )
    owned = received.reshape(block_rows, width)
    slot_index = lax.broadcasted_iota(jnp.int32, (nodes, slots), 1)
    live = (slot_index < got_counts.reshape(nodes, 1)).astype(jnp.float32).reshape(block_rows)
    live_wire = live.astype(jnp.bfloat16)
    density = tile_sums(owned, live, owned, live)[0]
    for shift_by in range(1, ROUNDS + 1):
        other_rows, other_flags = shifted((owned, live_wire), "join", shift_by)
        row_sums, col_sums = tile_sums(owned, live, other_rows, other_flags.astype(jnp.float32))
        density = density + row_sums + shifted(col_sums, "join", -shift_by)
    return live / (density + 1.0 - live)


def layer_kernel(slots, width, src_hbm, counts_hbm, out, src, counts, counts_row, held, snd, racc,
                 dacc, cacc, last, msg, got, live, insem, zsend, zrecv, lsend, lrecv, csend, crecv,
                 wsend, wrecv):
    gen, join = lax.axis_index("gen"), lax.axis_index("join")
    x, k, z, y = gen // 2, gen % 2, join // 2, join % 2
    inner = (z + 1) // 2 % 2
    flip = z + 1 - 2 * (z % 2)
    over = (z + 2) % 4
    far = 3 - z
    owners = 8
    rows = owners * slots
    tall = 4 * slots
    pieces = LAYERS * owners
    peers = [flip, far, over]
    sibling = (2 * x + 1 - k, join)
    x_near = (2 * (1 - x) + k, join)
    y_near = (gen, 2 * z + 1 - y)

    barrier = pltpu.get_barrier_semaphore()
    for peer in (
        (gen, 2 * flip + y), (gen, 2 * over + y), (gen, 2 * far + y), x_near, y_near, sibling
    ):
        pl.semaphore_signal(barrier, inc=1, device_id=peer, device_id_type=MESH)

    loads = [
        pltpu.make_async_copy(counts_hbm, counts, insem.at[LAYERS]),
        pltpu.make_async_copy(counts_hbm, counts_row, insem.at[LAYERS + 1]),
    ]
    for n, layer in enumerate([z] + peers):
        start = pl.multiple_of(layer * rows, rows)
        loads.append(
            pltpu.make_async_copy(src_hbm.at[pl.ds(start, rows)], src.at[n], insem.at[n])
        )
    for load in loads:
        load.start()

    def normalize(n, layer, b, into):
        start = pl.multiple_of(b * slots, slots)
        values = src[n, pl.ds(start, slots), :].astype(jnp.float32)
        spare = (counts[0, layer * owners + b]
                 - lax.broadcasted_iota(jnp.int32, (slots, 1), 0)).astype(jnp.float32)
        alive = jnp.clip(spare, 0.0, 1.0)
        factor = lax.rsqrt(jnp.mean(values * values, axis=1, keepdims=True) + 1e-06)
        into[...] = (values * (factor * (alive / math.sqrt(width)))).astype(jnp.bfloat16)

    def z_copy(slot, b):
        return pltpu.make_async_remote_copy(
            src_ref=snd.at[slot, b], dst_ref=held.at[slot + 1, b, OWN],
            send_sem=zsend.at[slot], recv_sem=zrecv.at[(slot + 1) * owners + b],
            device_id=(gen, 2 * peers[slot] + y), device_id_type=MESH,
        )

    def c_copy(slot):
        return pltpu.make_async_remote_copy(
            src_ref=live.at[0], dst_ref=live.at[slot + 1], send_sem=csend.at[slot],
            recv_sem=crecv.at[slot + 1], device_id=(gen, 2 * peers[slot] + y),
            device_id_type=MESH,
        )

    def l_copy(t, kind):
        d, b = t // owners, t % owners
        target = {XN: x_near, YN: y_near}[kind]
        way = kind // YN
        return pltpu.make_async_remote_copy(
            src_ref=held.at[d, b, OWN], dst_ref=held.at[d, b, kind],
            send_sem=lsend.at[way * LAYERS + d], recv_sem=lrecv.at[way * pieces + t],
            device_id=target, device_id_type=MESH,
        )

    def s_copy(t):
        d, b = t // owners, t % owners
        return pltpu.make_async_remote_copy(
            src_ref=held.at[d, b, pl.ds(OWN, 2)], dst_ref=held.at[d, b, pl.ds(SIB, 2)],
            send_sem=lsend.at[2 * LAYERS + d], recv_sem=lrecv.at[2 * pieces + t],
            device_id=sibling, device_id_type=MESH,
        )

    def spread(t):
        l_copy(t, XN).start()
        l_copy(t, YN).start()

    def arrive(t):
        d, b = t // owners, t % owners
        pltpu.make_async_remote_copy(
            src_ref=snd.at[0, 0], dst_ref=held.at[d, b, OWN],
            send_sem=zsend.at[0], recv_sem=zrecv.at[t],
            device_id=y_near, device_id_type=MESH,
        ).wait_recv()
        spread(t)

    def relay(t):
        l_copy(t, XN).wait_recv()
        s_copy(t).start()

    def normalize_slot(slot):
        def one(b, carry):
            normalize(slot + 1, peers[slot], b, snd.at[slot, b])
            return carry

        loads[slot + 3].wait()
        lax.fori_loop(0, owners, one, 0)

    def own_piece(b, carry):
        normalize(0, z, b, held.at[0, b, OWN])
        return carry

    for load in loads[:3]:
        load.wait()
    lax.fori_loop(0, owners, own_piece, 0)
    normalize_slot(0)
    normalize_slot(1)
    live[0] = jnp.zeros((8, 128), jnp.int32)
    live[0, 0:1, 0:32] = counts_row[...]
    pl.semaphore_wait(barrier, 6)

    for slot in range(3):
        c_copy(slot).start()

    def first(b, carry):
        @pl.when(inner == 1)
        def _():
            z_copy(1, b).start()

        z_copy(0, b).start()
        spread(b)
        return carry

    lax.fori_loop(0, owners, first, 0)
    normalize_slot(2)

    def second(b, carry):
        @pl.when(inner == 0)
        def _():
            z_copy(1, b).start()

        z_copy(2, b).start()
        return carry

    lax.fori_loop(0, owners, second, 0)
    racc[...] = jnp.zeros_like(racc)
    dacc[...] = jnp.zeros_like(dacc)
    cacc[...] = jnp.zeros_like(cacc)
    last[...] = jnp.zeros_like(last)

    lane_owner = lax.broadcasted_iota(jnp.int32, (1, rows), 1) // slots
    ones = jnp.ones((256, 128), jnp.bfloat16)
    diagonal = (
        lax.broadcasted_iota(jnp.int32, (128, 128), 0)
        == lax.broadcasted_iota(jnp.int32, (128, 128), 1)
    )

    turns = [(r, m) for r in range(2) for m in (0, 1, 2, 3, 5, 6, 7)]
    turn = lax.broadcasted_iota(jnp.int32, (1, len(turns) * slots), 1) // slots % 7
    turn = turn + turn // 4
    zero_one = jnp.minimum(turn, 1).astype(jnp.float32)

    def earlier(b, m):
        return (b - m) * ((b - m + owners) // owners)

    def settle(t):
        d, b = t // owners, t % owners
        sums = cacc[t % 2]
        high = sums.astype(jnp.bfloat16)
        low = (sums - high.astype(jnp.float32)).astype(jnp.bfloat16)
        summed = lax.dot_general(
            jnp.concatenate([high, low], axis=1), ones, (((1,), (0,)), ((), ())),
            preferred_element_type=jnp.float32,
        )
        line = jnp.concatenate([
            jnp.sum(jnp.where(diagonal, summed[c:c + 128, :], 0.0), axis=0, keepdims=True)
            for c in range(0, tall, 128)
        ], axis=1)
        msg[b, pl.ds(d, 1), :] = line
        for n, (r, m) in enumerate(turns):
            dacc[r, d, earlier(b, m), :, 0:slots] += last[t % 2, :, n * slots:(n + 1) * slots]

    def kernel_of(left, right):
        scores = lax.dot_general(
            left, right, (((1,), (1,)), ((), ())), preferred_element_type=jnp.float32
        )
        return jnp.exp2(scores * SCALE)

    def down(values):
        return jnp.sum(values.reshape(values.shape[0] // 8, 8, values.shape[1]), axis=0)

    def across(values):
        total = values[:, 0:128]
        for c in range(1, values.shape[1] // 128):
            total = total + values[:, 128 * c:128 * (c + 1)]
        return total

    def tile(d, b):
        left = held[d, b, 0:4].reshape(tall, width)
        total = jnp.zeros((tall, 128), jnp.float32)
        near = jnp.where(lane_owner != (b + 4) % owners, 1.0, 0.0)
        for i in range(d):
            for r, kind in enumerate((OWN, YN)):
                kernel = kernel_of(left, held[i, :, kind].reshape(rows, width))
                racc[r, i] += down(kernel) * near
                total = total + across(kernel * near)
        right = jnp.concatenate(
            [held[d, earlier(b, m), (OWN, YN)[r]] for r, m in turns], axis=0
        )
        kernel = kernel_of(left, right)
        use = jnp.where(turn <= b, 1.0, 0.0)
        last[(d * owners + b) % 2] = down(kernel) * use
        total = total + across(kernel * (use * zero_one))
        cacc[(d * owners + b) % 2] = total

    def follow(d, b, ahead, next_up):
        t = d * owners + b
        if ahead:
            arrive(t + 4)
        if next_up:
            relay(t + 1)
        l_copy(t, YN).wait_recv()
        s_copy(t).wait_recv()
        settle((t + pieces - 1) % pieces)
        tile(d, b)

    relay(0)
    for d in range(LAYERS):
        spans = {0: (0, 4, 8), 1: (0, 8), 2: (0, 8), 3: (0, 4, 7, 8)}[d]
        for start, stop in zip(spans, spans[1:]):
            ahead = start >= 4 if d == 0 else d < 3 or start == 0

            def step(b, carry):
                follow(d, b, ahead, stop < owners or d < 3)
                return carry

            lax.fori_loop(start, stop, step, 0)
        if d == 1:
            for place in range(1, LAYERS):
                pltpu.make_async_remote_copy(
                    src_ref=live.at[0], dst_ref=live.at[place], send_sem=csend.at[0],
                    recv_sem=crecv.at[place], device_id=y_near, device_id_type=MESH,
                ).wait_recv()
            lane = lax.broadcasted_iota(jnp.int32, (owners, 128), 1)
            mine = owners * z + lax.broadcasted_iota(jnp.int32, (owners, 128), 0)
            across_of = owners * z + (4 + lax.broadcasted_iota(jnp.int32, (owners, 128), 0)) % owners
            group = (lane >= owners * z) & (lane < owners * z + owners) & (lane != across_of)
            slot_index = lax.broadcasted_iota(jnp.int32, (owners, slots), 1).astype(jnp.float32)
            dead = jnp.zeros((owners, 128), jnp.float32)
            for place in range(LAYERS):
                filled = jnp.broadcast_to(live[place, 0:1, :].astype(jnp.float32), (owners, 128))
                limit = jnp.sum(jnp.where(lane == mine, filled, 0.0), axis=1, keepdims=True)
                flags = jnp.where(slot_index < limit, 1.0, 0.0)
                for j in range(owners):
                    msg[j, 4 + place:5 + place, 2 * slots:3 * slots] = flags[j:j + 1, :]
                dead = dead + jnp.where(group, float(slots) - filled, 0.0)
            missing = jnp.broadcast_to(jnp.sum(dead, axis=1, keepdims=True), (owners, slots))
            for j in range(owners):
                msg[j, 4:5, 3 * slots:4 * slots] = missing[j:j + 1, :]

    settle(pieces - 1)
    spot = 2 * gen + y

    def w_copy(j):
        return pltpu.make_async_remote_copy(
            src_ref=msg.at[j], dst_ref=got.at[spot], send_sem=wsend.at[j],
            recv_sem=wrecv.at[spot], device_id=(z, j), device_id_type=MESH,
        )

    def send(j, carry):
        @pl.when(z * owners + j != gen * owners + join)
        def _():
            w_copy(j).start()

        @pl.when(z * owners + j == gen * owners + join)
        def _():
            got[spot] = msg[j]

        return carry

    lines = [
        (r, d, jnp.sum(racc[r, d], axis=0, keepdims=True)) for r in range(2) for d in range(LAYERS)
    ]
    for j in range(owners):
        for r, d, line in lines:
            extra = jnp.sum(dacc[r, d, j, :, 0:slots], axis=0, keepdims=True)
            msg[j, 4 + d:5 + d, r * slots:(1 + r) * slots] = (
                line[:, j * slots:(j + 1) * slots] + extra
            )
        send(j, 0)

    def receive(i, carry):
        @pl.when((i // 2) * owners + 2 * gen + i % 2 != gen * owners + join)
        def _():
            pltpu.make_async_remote_copy(
                src_ref=msg.at[0], dst_ref=got.at[i], send_sem=wsend.at[0],
                recv_sem=wrecv.at[i], device_id=y_near, device_id_type=MESH,
            ).wait_recv()

        return carry

    lax.fori_loop(0, owners, receive, 0)

    missing = got[0, 4:5, 3 * slots:4 * slots]
    for q in range(1, owners):
        missing = missing + got[q, 4:5, 3 * slots:4 * slots]
    g_order = [gen, gen + 1 - 2 * (gen % 2), 3 - gen, (gen + 2) % 4]
    for pair in range(4):
        halves = []
        for half in range(2):
            q = 2 * pair + half

            def field(sender, n):
                row, lane = LAYERS * (n // 4), slots * (n % 4)
                return got[sender, row:row + LAYERS, lane:lane + slots]

            total = field(q, OWN) + field(q ^ 4, XN) + field(q ^ 2, SIB) + field(q ^ 6, XS)
            total = total + field(q, 4) + field(q ^ 1, 5)
            flags = field(q, 6)
            density = (total - missing) * math.exp(-8.0)
            halves.append(flags / (density + 1.0 - flags))
        both = jnp.concatenate(halves, axis=1)
        for d in range(LAYERS):
            out[pl.ds(LAYERS * pair + g_order[d], 1), :] = both[d:d + 1, :]

    def sent(j, carry):
        @pl.when(z * owners + j != gen * owners + join)
        def _():
            w_copy(j).wait_send()

        return carry

    lax.fori_loop(0, owners, sent, 0)
    for slot in range(3):
        c_copy(slot).wait_send()
        pltpu.make_async_remote_copy(
            src_ref=snd.at[slot], dst_ref=snd.at[slot], send_sem=zsend.at[slot],
            recv_sem=zrecv.at[0], device_id=y_near, device_id_type=MESH,
        ).wait_send()
    for d in range(LAYERS):
        for way in range(3):
            place = (pl.ds(OWN, 1), pl.ds(OWN, 1), pl.ds(OWN, 2))[way]
            pltpu.make_async_remote_copy(
                src_ref=held.at[d, :, place], dst_ref=held.at[d, :, place],
                send_sem=lsend.at[way * LAYERS + d], recv_sem=lrecv.at[0],
                device_id=y_near, device_id_type=MESH,
            ).wait_send()


def layer_body(src_emb, counts):
    block, width = src_emb.shape
    owners = 8
    slots = block // (LAYERS * owners)
    vmem = pl.BlockSpec(memory_space=pltpu.VMEM)
    weights = pl.pallas_call(
        lambda *refs: layer_kernel(slots, width, *refs),
        out_shape=jax.ShapeDtypeStruct((block // 128, 128), jnp.float32),
        in_specs=[pl.BlockSpec(memory_space=pl.ANY)] * 2,
        out_specs=vmem,
        scratch_shapes=[
            pltpu.VMEM((LAYERS, owners * slots, width), jnp.bfloat16),
            pltpu.SMEM((1, 32), jnp.int32),
            pltpu.VMEM((1, 32), jnp.int32),
            pltpu.VMEM((LAYERS, owners, 5, slots, width), jnp.bfloat16),
            pltpu.VMEM((LAYERS - 1, owners, slots, width), jnp.bfloat16),
            pltpu.VMEM((2, LAYERS, 8, owners * slots), jnp.float32),
            pltpu.VMEM((2, LAYERS, owners, 8, 128), jnp.float32),
            pltpu.VMEM((2, 4 * slots, 128), jnp.float32),
            pltpu.VMEM((2, 8, 14 * slots), jnp.float32),
            pltpu.VMEM((owners, 8, 4 * slots), jnp.float32),
            pltpu.VMEM((owners, 8, 4 * slots), jnp.float32),
            pltpu.VMEM((LAYERS, 8, 128), jnp.int32),
            pltpu.SemaphoreType.DMA((LAYERS + 2,)),
            pltpu.SemaphoreType.DMA((3,)),
            pltpu.SemaphoreType.DMA((LAYERS * owners,)),
            pltpu.SemaphoreType.DMA((3 * LAYERS,)),
            pltpu.SemaphoreType.DMA((3 * LAYERS * owners,)),
            pltpu.SemaphoreType.DMA((3,)),
            pltpu.SemaphoreType.DMA((LAYERS,)),
            pltpu.SemaphoreType.DMA((owners,)),
            pltpu.SemaphoreType.DMA((owners,)),
        ],
        compiler_params=pltpu.CompilerParams(
            collective_id=0, has_side_effects=True, vmem_limit_bytes=56 * 2**20
        ),
        name="layer_kernel",
    )(src_emb, counts)
    return weights.reshape(block)


def solution(mesh):
    in_specs = (P(("gen", "join"), None), P(("gen", "join"), None))
    out_specs = P(("gen", "join"))
    fits = mesh.shape["gen"] == 4 and mesh.shape["join"] == 8
    body = layer_body if fits else ring_body
    return jax.shard_map(body, mesh=mesh, in_specs=in_specs, out_specs=out_specs, check_vma=False)
```
